32 devices in a mesh: group: 2 (over y), dp: 4 (over z), chan: 4 (over x, core).
Axes of the slice: x: 2, y: 2, z: 4, core: 2. Of those that a mesh axis runs over, the one named last changes fastest.
Arguments:
- audio: bfloat16 [8, 8, 512], P(None, ('group', 'dp')), parts along dimension 1, may hold values from -3 to 3
- mel: bfloat16 [640, 8, 512], P(None, ('group', 'dp')), parts along dimension 1, may hold values from -5 to 5
- crop_len: int32 [8, 4], P('group'), parts along dimension 0, may hold values from 0 to 128, as said below
- pack_offset: int32 [8, 4], P('group'), parts along dimension 0, may hold values from 0 to 256, as said below
- low_mix: float32 [2, 8, 8], replicated, may hold values from -1.5 to 1.5
- up_mix: float32 [2, 8, 8], replicated, may hold values from -1.5 to 1.5
- log_scale: float32 [2, 8], replicated, may hold values from -0.5 to 0.5
- w_start: float32 [2, 4, 512], replicated, may hold values from -3 to 3
- w_in: bfloat16 [2, 2, 512, 1536], P(None, None, 'chan'), may hold values from -0.15625 to 0.15625
- w_cond: bfloat16 [2, 2, 512, 640], P(None, None, 'chan'), may hold values from -0.25 to 0.25
- w_skip: bfloat16 [2, 512, 512], P(None, 'chan'), may hold values from -0.25 to 0.25
- w_end: float32 [2, 8, 512], replicated, may hold values from -0.125 to 0.125
Outputs:
- g_start: float32 [4, 4, 512], P('group', None, 'dp'), parts along dimension 0
- g_in: float32 [4, 2, 512, 1536], P('group', None, 'chan', 'dp'), parts along dimension 0
- g_cond: float32 [4, 2, 512, 640], P('group', None, 'chan', 'dp'), parts along dimension 0
- g_skip: float32 [4, 512, 512], P('group', 'chan', 'dp'), parts along dimension 0
- g_end: float32 [4, 8, 512], P('group', None, 'dp'), parts along dimension 0
The draws below stay inside these ranges and needn't reach their ends.
There are 2 independent parts, one for each index of `group`. The reference program is written for one: setup_inputs(seed, part) draws one part's arguments, and reference() takes and returns one part's arrays. A program takes and returns all parts, laid end to end along the dimension named above; an argument that names none is the same for every part. Nothing has to cross between parts.
Inputs may be any that keep to these rules, and one draw needn't show every extreme that they name: Every row o sums to 256, every row holds an entry equal to 128 and one equal to 0; slots k >= crop_len[o, l] of a pair carry no frame. For each owner o the ranges pack_offset[o, l] to pack_offset[o, l] + crop_len[o, l] - 1 are disjoint and cover all 256 rows, in an order drawn for each owner; the empty crop has offset 256.
All inputs are finite; a program needn't handle non-finite values.
Results may differ from the reference program's by a relative error of at most 0.015.
Values may be sent and summed in bfloat16 or wider, within the bound.
A program may use at most 64 MiB of HBM per device.

```python
import math
import jax
import jax.numpy as jnp
from jax import lax

G = 8
H = 4
R = 512
MEL = 640
NFLOW = 2
PACK = 256
CAP = 128
ROWS = 1024
N_DP = 4
N_CHAN = 4


def crop_tables(key):
    base_key = jax.random.fold_in(key, 11)
    key_delta, key_place, key_order = jax.random.split(base_key, 3)
    mean_len = CAP // 2
    pairs_count = N_DP // 2
    delta = jax.random.randint(key_delta, (N_DP, pairs_count), -(mean_len - 1), mean_len, dtype=jnp.int32)
    delta = delta.at[:, 0].set(mean_len)
    values = jnp.concatenate([mean_len + delta, mean_len - delta], axis=1).astype(jnp.int32)
    placing = jax.vmap(lambda sub_key: jax.random.permutation(sub_key, N_DP))(jax.random.split(key_place, N_DP))
    lengths = jnp.take_along_axis(values, placing, axis=1).astype(jnp.int32)
    ordering = jax.vmap(lambda sub_key: jax.random.permutation(sub_key, N_DP))(jax.random.split(key_order, N_DP))
    first_order = jnp.take_along_axis(lengths, ordering, axis=1)
    empty_last = jnp.argsort((first_order == 0).astype(jnp.int32), axis=1, stable=True).astype(jnp.int32)
    ordering = jnp.take_along_axis(ordering, empty_last, axis=1).astype(jnp.int32)
    in_order = jnp.take_along_axis(lengths, ordering, axis=1)
    before = (jnp.cumsum(in_order, axis=1) - in_order).astype(jnp.int32)
    offsets = jax.vmap(lambda slots, starts: jnp.zeros((N_DP,), jnp.int32).at[slots].set(starts))(ordering, before)
    return (lengths, offsets.astype(jnp.int32))


def draw_crop_len(key, part):
    return crop_tables(key)[0]


def draw_pack_offset(key, part):
    return crop_tables(key)[1]


def block_scale(stream_key, extent, shards, low, largest):
    def one(position, blocks):
        steps = jax.random.uniform(jax.random.fold_in(jax.random.fold_in(stream_key, 6), position), (blocks,), jnp.float32, low / len(shards), largest / len(shards))
        return jnp.repeat(jnp.exp(steps), extent[position] // blocks).reshape((-1,) + (1,) * (len(extent) - position - 1))

    factor_of = one(*shards[0])
    for cut in shards[1:]:
        factor_of = factor_of * one(*cut)
    return factor_of


def noise(key, dims, spread, reach, pieces=(), kind=jnp.bfloat16):
    entries = jax.random.normal(key, dims, jnp.float32) * spread
    if len(pieces) > 0:
        entries = block_scale(key, dims, pieces, -0.22, 0.18) * entries
    return jnp.clip(entries, min=-reach, max=reach).astype(kind)


def setup_inputs(seed: int = 0, part: int = 0) -> dict:
    keys = jax.random.split(jax.random.key(seed), 13)
    part_splits = jax.random.split(jax.random.fold_in(keys[12], part), 13)
    return {
        "audio": noise(part_splits[0], (G, N_DP, N_DP * CAP), 0.5, 3.0, ((1, 4),)),
        "mel": noise(part_splits[1], (MEL, N_DP, N_DP * CAP), 1.0, 5.0, ((1, 4),)),
        "crop_len": draw_crop_len(jax.random.fold_in(jax.random.fold_in(keys[12], part), 71), part),
        "pack_offset": draw_pack_offset(jax.random.fold_in(jax.random.fold_in(keys[12], part), 71), part),
        "low_mix": noise(keys[4], (NFLOW, G, G), 0.3, 1.5, (), jnp.float32),
        "up_mix": noise(keys[5], (NFLOW, G, G), 0.3, 1.5, (), jnp.float32),
        "log_scale": jnp.clip(jax.random.uniform(keys[6], (NFLOW, G), jnp.float32, -0.5, 0.5), -0.5, 0.5),
        "w_start": noise(keys[7], (NFLOW, H, R), H ** -0.5, 3.0, (), jnp.float32),
        "w_in": noise(keys[8], (NFLOW, 2, R, 3 * R), (3 * R) ** -0.5, 0.15625, ((2, 4),)),
        "w_cond": noise(keys[9], (NFLOW, 2, R, MEL), MEL ** -0.5, 0.25, ((2, 4),)),
        "w_skip": noise(keys[10], (NFLOW, R, R), R ** -0.5, 0.25, ((1, 4),)),
        "w_end": noise(keys[11], (NFLOW, 2 * H, R), (4 * R) ** -0.5, 0.125, (), jnp.float32),
    }


HIGH = lax.Precision.HIGHEST

def shift_right(values):
    return jnp.pad(values, ((0, 0), (1, 0)))[:, :-1]

def shift_left(values):
    return jnp.pad(values, ((0, 0), (0, 1)))[:, 1:]

def contract_first(a_mat, b_mat, precision=None):
    return lax.dot_general(a_mat, b_mat, (((0,), (0,)), ((), ())), precision=precision, preferred_element_type=jnp.float32)

def contract_last(a_mat, b_mat, precision=None):
    return lax.dot_general(a_mat, b_mat, (((1,), (1,)), ((), ())), precision=precision, preferred_element_type=jnp.float32)

def matmul(a_mat, b_mat, precision=None):
    return jnp.dot(a_mat, b_mat, precision=precision, preferred_element_type=jnp.float32)

def rounded(values):
    return lax.optimization_barrier(values.astype(jnp.bfloat16)).astype(jnp.float32)

def mix_matrix(low_part, upper_part, log_diag):
    identity = jnp.eye(low_part.shape[0], dtype=jnp.float32)
    lower_full = identity + jnp.tril(low_part, -1)
    upper_full = jnp.triu(upper_part, 1) + jnp.diag(jnp.exp(log_diag))
    return jnp.dot(lower_full, upper_full, precision=HIGH)

def pack_layout(lengths, offsets, pack_width):
    row_ids = jnp.arange(pack_width, dtype=jnp.int32)
    inside = (row_ids[:, None] >= offsets[None, :]) & (row_ids[:, None] < offsets[None, :] + lengths[None, :])
    loaders = jnp.arange(lengths.shape[0], dtype=jnp.int32)
    crop_id = lax.optimization_barrier(jnp.sum(jnp.where(inside, loaders[None, :], 0), axis=1)).astype(jnp.int32)
    row_start = lax.optimization_barrier(jnp.sum(jnp.where(inside, offsets[None, :], 0), axis=1)).astype(jnp.int32)
    return (crop_id, row_ids - row_start)

def pack_grads(x_state, packed_mel, prev_mask, next_mask, mixes, w_start, w_in, w_cond, w_skip, w_end, obj_scale):
    block_width = R // N_CHAN
    saved = []
    for flow_idx in range(NFLOW):
        mixing = mixes[flow_idx]
        x_state = matmul(mixing, x_state, HIGH)
        first_half = x_state[:H]
        second = x_state[H:]
        hidden = contract_first(w_start[flow_idx], first_half, HIGH).astype(jnp.bfloat16)
        stacked = jnp.concatenate([shift_right(hidden) * prev_mask.astype(jnp.bfloat16), hidden, shift_left(hidden) * next_mask.astype(jnp.bfloat16)], axis=0)
        skip_full = jnp.zeros((R, x_state.shape[1]), jnp.float32)
        blocks = []
        for block_idx in range(N_CHAN):
            lead = block_idx * block_width
            pre_tanh = matmul(w_in[flow_idx, 0, lead:lead + block_width], stacked) + matmul(w_cond[flow_idx, 0, lead:lead + block_width], packed_mel)
            pre_sigm = matmul(w_in[flow_idx, 1, lead:lead + block_width], stacked) + matmul(w_cond[flow_idx, 1, lead:lead + block_width], packed_mel)
            tanh_val = jnp.tanh(pre_tanh)
            sigm_val = jax.nn.sigmoid(pre_sigm)
            gated_act = (tanh_val * sigm_val).astype(jnp.bfloat16)
            skip_full = skip_full + rounded(contract_first(w_skip[flow_idx, lead:lead + block_width], gated_act))
            blocks.append((tanh_val, sigm_val, gated_act))
        coupling = matmul(w_end[flow_idx], skip_full, HIGH)
        exp_gain = jnp.exp(coupling[:H])
        saved.append((mixing, first_half, second, stacked, blocks, skip_full, exp_gain))
        x_state = jnp.concatenate([first_half, exp_gain * second + coupling[H:]], axis=0)
    grad_state = obj_scale * x_state
    collected = [None] * NFLOW
    for flow_idx in reversed(range(NFLOW)):
        mixing, first_half, second, stacked, blocks, skip_full, exp_gain = saved[flow_idx]
        grad_first = grad_state[:H]
        grad_second = grad_state[H:]
        grad_log = grad_second * exp_gain * second - obj_scale
        grad_coupling = jnp.concatenate([grad_log, grad_second], axis=0)
        end_term = contract_last(grad_coupling, skip_full, HIGH)
        grad_skip = contract_first(w_end[flow_idx], grad_coupling, HIGH).astype(jnp.bfloat16)
        grad_hidden = jnp.zeros((R, x_state.shape[1]), jnp.float32)
        in_list, cond_list, skip_list = ([], [], [])
        for block_idx in range(N_CHAN):
            lead = block_idx * block_width
            tanh_val, sigm_val, gated_act = blocks[block_idx]
            grad_gated = matmul(w_skip[flow_idx, lead:lead + block_width], grad_skip)
            skip_list.append(contract_last(gated_act, grad_skip))
            grad_tanh = (grad_gated * sigm_val * (1.0 - tanh_val * tanh_val)).astype(jnp.bfloat16)
            grad_sigm = (grad_gated * tanh_val * sigm_val * (1.0 - sigm_val)).astype(jnp.bfloat16)
            in_list.append(jnp.stack([contract_last(grad_tanh, stacked), contract_last(grad_sigm, stacked)]))
            cond_list.append(jnp.stack([contract_last(grad_tanh, packed_mel), contract_last(grad_sigm, packed_mel)]))
            grad_stacked = contract_first(w_in[flow_idx, 0, lead:lead + block_width], grad_tanh) + contract_first(w_in[flow_idx, 1, lead:lead + block_width], grad_sigm)
            grad_prev = grad_stacked[:R]
            grad_mid = grad_stacked[R:2 * R]
            grad_next = grad_stacked[2 * R:]
            hidden_part = grad_mid + shift_left(grad_prev * prev_mask) + shift_right(grad_next * next_mask)
            grad_hidden = grad_hidden + rounded(hidden_part)
        start_term = contract_last(first_half, grad_hidden, HIGH)
        grad_first = grad_first + matmul(w_start[flow_idx], grad_hidden, HIGH)
        grad_state = matmul(mixing.T, jnp.concatenate([grad_first, grad_second * exp_gain], axis=0), HIGH)
        collected[flow_idx] = (start_term, jnp.concatenate(in_list, axis=1), jnp.concatenate(cond_list, axis=1), jnp.concatenate(skip_list, axis=0), end_term)
    return tuple((jnp.stack([collected[flow_num][item_num] for flow_num in range(NFLOW)]) for item_num in range(5)))

def reference(audio, mel, crop_len, pack_offset, low_mix, up_mix, log_scale, w_start, w_in, w_cond, w_skip, w_end):
    mixes = [mix_matrix(low_mix[flow_idx], up_mix[flow_idx], log_scale[flow_idx]) for flow_idx in range(NFLOW)]
    obj_scale = 8.0 / math.sqrt(ROWS)

    def one_pack(totals, owner):
        lengths = crop_len[owner]
        offsets = pack_offset[owner]
        crop_id, within = pack_layout(lengths, offsets, PACK)
        columns = (owner * CAP + within).astype(jnp.int32)
        x_state = audio[:, crop_id, columns].astype(jnp.float32)
        packed_mel = mel[:, crop_id, columns]
        same_prev = jnp.concatenate([jnp.zeros((1,), bool), crop_id[1:] == crop_id[:-1]])
        same_next = jnp.concatenate([crop_id[:-1] == crop_id[1:], jnp.zeros((1,), bool)])
        prev_mask = same_prev.astype(jnp.float32)[None, :]
        next_mask = same_next.astype(jnp.float32)[None, :]
        grads = pack_grads(x_state, packed_mel, prev_mask, next_mask, mixes, w_start, w_in, w_cond, w_skip, w_end, obj_scale)
        return (tuple((total + term for total, term in zip(totals, grads))), None)
    init = (jnp.zeros((NFLOW, H, R), jnp.float32), jnp.zeros((NFLOW, 2, R, 3 * R), jnp.float32), jnp.zeros((NFLOW, 2, R, MEL), jnp.float32), jnp.zeros((NFLOW, R, R), jnp.float32), jnp.zeros((NFLOW, 2 * H, R), jnp.float32))
    totals, _ = lax.scan(one_pack, init, jnp.arange(N_DP, dtype=jnp.int32))
    return (totals[0], totals[1], totals[2], totals[3], totals[4])
```

```python
import functools
import math

import jax
import jax.numpy as jnp
from jax import lax
from jax.experimental import pallas as pl
from jax.experimental.pallas import tpu as pltpu
from jax.sharding import PartitionSpec as P

H = 4
NFLOW = 2
PACK = 256
MESH = pl.DeviceIdType.MESH
F32 = jnp.float32
BF16 = jnp.bfloat16


def dot(a, b, dims):
    return lax.dot_general(a, b, (dims, ((), ())), preferred_element_type=F32)


def halves(a):
    high = a.astype(BF16).astype(F32)
    return high, a - high


def cat_left(a):
    high, low = halves(a)
    return jnp.concatenate([high, high, low], axis=0).astype(BF16)


def cat_right(b):
    high, low = halves(b)
    return jnp.concatenate([high, low, high], axis=0).astype(BF16)


def dot_tn(a, b):
    return dot(cat_left(a), cat_right(b), ((0,), (0,)))


def cat_rows(a):
    high, low = halves(a)
    return jnp.concatenate([high, low], axis=0).astype(BF16)


def fold_rows(r):
    half = r.shape[0] // 2
    return r[:half] + r[half:]


def columns(read, base, start, size, full):
    if size % 128 == 0:
        return read(pl.ds(pl.multiple_of(base + start, 128), size))
    row = lax.broadcasted_iota(jnp.int32, (full, size), 0)
    col = lax.broadcasted_iota(jnp.int32, (full, size), 1)
    pick = jnp.where(row == col + start, 1.0, 0.0).astype(BF16)
    return dot(read(slice(base, base + full)), pick, ((1,), (0,))).astype(BF16)


def columns_f32(read, start, size, full):
    if size % 128 == 0:
        return read(pl.ds(pl.multiple_of(start, 128), size))
    row = lax.broadcasted_iota(jnp.int32, (full, size), 0)
    col = lax.broadcasted_iota(jnp.int32, (full, size), 1)
    pick = jnp.where(row == col + start, 1.0, 0.0).astype(BF16)
    return fold_rows(dot(cat_rows(read(slice(None))), pick, ((1,), (0,))))


def kernel(
    n_dp,
    n_chan,
    len_hbm,
    audio_hbm,
    low_hbm,
    up_hbm,
    scale_hbm,
    w_start_hbm,
    w_end_hbm,
    mel_hbm,
    w_in_hbm,
    w_cond_hbm,
    w_skip_hbm,
    o_start,
    o_in,
    o_cond,
    o_skip,
    o_end,
    len_ref,
    audio_ref,
    low_ref,
    up_ref,
    scale_ref,
    w_start_ref,
    w_end_ref,
    mel,
    w_in,
    w_cond,
    w_skip,
    w_first,
    basis,
    cond,
    chan_buf,
    fin_buf,
    sum_buf,
    snd_buf,
    rcv_buf,
    fwd_buf,
    load_sem,
    chan_send,
    chan_recv,
    sum_send,
    sum_recv,
    cond_send,
    cond_recv,
):
    slots = audio_ref.shape[1]
    cap = slots // n_dp
    width = w_in_hbm.shape[2]
    res = w_end_ref.shape[2]
    mel_rows = mel_hbm.shape[0] // n_dp
    res_size = o_skip.shape[2]
    in_size = o_in.shape[3]
    obj_scale = 8.0 / math.sqrt(n_dp * PACK)
    me = lax.axis_index("dp")
    chan = lax.axis_index("chan")

    barrier = pltpu.get_barrier_semaphore()
    for step in range(1, n_chan):
        peer = lax.rem(chan + step, n_chan)
        pl.semaphore_signal(barrier, inc=1, device_id={"chan": peer}, device_id_type=MESH)
    for step in range(1, n_dp):
        peer = lax.rem(me + step, n_dp)
        pl.semaphore_signal(barrier, inc=1, device_id={"dp": peer}, device_id_type=MESH)

    pairs = {
        "start": (w_start_hbm, w_start_ref),
        "in0": (w_in_hbm.at[0], w_in.at[0]),
        "len": (len_hbm, len_ref),
        "audio": (audio_hbm, audio_ref),
        "low": (low_hbm, low_ref),
        "up": (up_hbm, up_ref),
        "scale": (scale_hbm, scale_ref),
        "end": (w_end_hbm, w_end_ref),
        "skip": (w_skip_hbm, w_skip),
        "mel": (mel_hbm, mel),
        "cond0": (w_cond_hbm.at[0], w_cond.at[0]),
        "in1": (w_in_hbm.at[1], w_in.at[1]),
        "cond1": (w_cond_hbm.at[1], w_cond.at[1]),
    }
    loads = {
        key: pltpu.make_async_copy(src, dst, load_sem.at[at])
        for at, (key, (src, dst)) in enumerate(pairs.items())
    }
    for load in loads.values():
        load.start()

    def chan_start(buf, phase, value):
        buf[chan] = value
        copies = [
            pltpu.make_async_remote_copy(
                src_ref=buf.at[chan],
                dst_ref=buf.at[chan],
                send_sem=chan_send.at[phase, step],
                recv_sem=chan_recv.at[phase, step],
                device_id={"chan": lax.rem(chan + step, n_chan)},
                device_id_type=MESH,
            )
            for step in range(1, n_chan)
        ]
        for copy in copies:
            copy.start()
        pending.extend(copies)
        return copies

    def chan_finish(buf, copies):
        for copy in copies:
            copy.wait_recv()
        total = buf[0]
        for block in range(1, n_chan):
            total = total + buf[block]
        return total

    pending = []
    w_first[...] = jnp.zeros(w_first.shape, F32)
    basis[...] = jnp.zeros(basis.shape, F32)

    for key in ("len", "audio", "low", "up", "scale"):
        loads[key].wait()
    column = lax.broadcasted_iota(jnp.int32, (8, slots), 1)
    owner = column // cap
    within = column - owner * cap
    lens = jnp.zeros((8, slots), jnp.int32)
    for block in range(n_dp):
        lens = jnp.where(owner == block, len_ref[block, me], lens)
    valid = within < lens
    prev_mask = valid & (within >= 1)
    next_mask = within + 1 < lens

    row8 = lax.broadcasted_iota(jnp.int32, (8, 8), 0)
    col8 = lax.broadcasted_iota(jnp.int32, (8, 8), 1)
    mixes = []
    for f in range(NFLOW):
        lower = jnp.where(row8 > col8, low_ref[f], jnp.where(row8 == col8, 1.0, 0.0))
        diag = jnp.broadcast_to(jnp.exp(scale_ref[f : f + 1, :]), (8, 8))
        upper = jnp.where(row8 < col8, up_ref[f], jnp.where(row8 == col8, diag, 0.0))
        mixing = lower[:, 0:1] * upper[0:1, :]
        for k in range(1, 8):
            mixing = mixing + lower[:, k : k + 1] * upper[k : k + 1, :]
        mixes.append(mixing)

    def mix(f, x):
        mixing = mixes[f]
        mixed = mixing[:, 0:1] * x[0:1, :]
        for k in range(1, 8):
            mixed = mixed + mixing[:, k : k + 1] * x[k : k + 1, :]
        return mixed

    w_eff = [None] * NFLOW
    b_skip = [None] * NFLOW

    def precompute(f):
        loads["in%d" % f].wait()
        start16 = cat_rows(w_first[f])
        taps = []
        for tap in range(3):
            block = w_in[f, :, :, tap * res : (tap + 1) * res].reshape(2 * width, res)
            taps.append(fold_rows(dot(start16, block, ((1,), (1,)))))
        w_eff[f] = jnp.concatenate(taps, axis=0)
        if f == 0:
            loads["end"].wait()
            loads["skip"].wait()
        b_skip[f] = fold_rows(dot(cat_rows(w_end_ref[f]), w_skip[f], ((1,), (1,))))
        if f == 0:
            loads["mel"].wait()
        loads["cond%d" % f].wait()
        every = w_cond[f].reshape(2 * width, w_cond.shape[3])
        cond[f] = dot(every, mel[...], ((1,), (0,)))

    x_state = jnp.where(valid, audio_ref[...].astype(F32), 0.0)
    loads["start"].wait()
    for f in range(NFLOW):
        w_first[f, :H] = w_start_ref[f]
    precompute(0)
    saved = []
    for f in range(NFLOW):
        mixed = mix(f, x_state)
        stacked = jnp.concatenate(
            [
                jnp.where(prev_mask, pltpu.roll(mixed, 1, 1), 0.0),
                mixed,
                jnp.where(next_mask, pltpu.roll(mixed, slots - 1, 1), 0.0),
            ],
            axis=0,
        )
        pre = dot_tn(w_eff[f], stacked) + cond[f]
        tanh_val = jnp.tanh(pre[:width])
        sigm_val = 0.5 * jnp.tanh(0.5 * pre[width:]) + 0.5
        gated = (tanh_val * sigm_val).astype(BF16)
        part = fold_rows(dot(cat_rows(b_skip[f]), gated, ((1,), (0,))))
        if f == 0:
            pl.semaphore_wait(barrier, n_chan + n_dp - 2)
        copies = chan_start(chan_buf.at[f], f, part)
        if f == 0:
            precompute(1)
            for g in range(NFLOW):
                for tap in range(3):
                    basis[g, tap * H : tap * H + H, tap * res : (tap + 1) * res] = w_start_ref[g]
        slope_tanh = sigm_val * (1.0 - tanh_val * tanh_val)
        slope_sigm = tanh_val * sigm_val * (1.0 - sigm_val)
        coupling = chan_finish(chan_buf.at[f], copies)
        gain = jnp.exp(coupling[:H])
        second = mixed[H:]
        saved.append((mixed, stacked, slope_tanh, slope_sigm, gated, gain))
        x_state = jnp.where(
            valid, jnp.concatenate([mixed[:H], gain * second + coupling[H:]], axis=0), 0.0
        )

    side = me + 1 - 2 * lax.rem(me, 2)
    far = lax.rem(me + 2, n_dp)
    if n_dp == 4:
        routes = [(side, lax.rem(side + 2, n_dp)), (side, side)]
    else:
        routes = [(lax.rem(me + step, n_dp),) * 2 for step in range(1, n_dp)]

    def block_rows(block):
        return pl.ds(pl.multiple_of(block * mel_rows, 16), mel_rows)

    def cond_copy(f, source, slot, peer):
        return pltpu.make_async_remote_copy(
            src_ref=source,
            dst_ref=rcv_buf.at[f, slot],
            send_sem=cond_send.at[f, slot],
            recv_sem=cond_recv.at[f, slot],
            device_id={"dp": peer},
            device_id_type=MESH,
        )

    def cond_part(f, both, block):
        rows = block_rows(block)
        snd_buf[f, rows, :] = dot(mel[rows, :], both, ((1,), (1,))).astype(BF16)

    def cond_relay(f):
        if n_dp != 4:
            return
        cond_copies[f][0].wait_recv()
        total = snd_buf[f, block_rows(far), :].astype(F32) + rcv_buf[f, 0].astype(F32)
        fwd_buf[f] = total.astype(BF16)
        copy = cond_copy(f, fwd_buf.at[f], 2, far)
        copy.start()
        cond_copies[f].append(copy)
        pending.append(copy)

    grad_state = obj_scale * x_state
    sum_copies = [None] * NFLOW
    cond_copies = [None] * NFLOW
    for f in reversed(range(NFLOW)):
        mixed, stacked, slope_tanh, slope_sigm, gated, gain = saved[f]
        grad_second = grad_state[H:]
        grad_log = grad_second * gain * mixed[H:] - obj_scale
        grad_coupling = jnp.where(
            valid, jnp.concatenate([grad_log, grad_second], axis=0), 0.0
        )
        grad_gated = dot_tn(b_skip[f], grad_coupling)
        grad_tanh = (grad_gated * slope_tanh).astype(BF16)
        grad_sigm = (grad_gated * slope_sigm).astype(BF16)
        both = jnp.concatenate([grad_tanh, grad_sigm], axis=0)
        if f > 0:
            back = fold_rows(dot(cat_rows(w_eff[f]), both, ((1,), (0,))))
            part = (
                back[8:16]
                + pltpu.roll(jnp.where(prev_mask, back[0:8], 0.0), slots - 1, 1)
                + pltpu.roll(jnp.where(next_mask, back[16:24], 0.0), 1, 1)
            )
            copies = chan_start(chan_buf.at[NFLOW + f - 1], NFLOW + f - 1, part)
        left = cat_rows(jnp.concatenate([stacked, grad_coupling], axis=0))
        values = jnp.concatenate([both, gated], axis=0)
        r = fold_rows(dot(left, values, ((1,), (1,))))
        n_part = jnp.concatenate([r[0:4], r[8:12], r[16:20], r[20:24]], axis=0)[:, : 2 * width]
        m_part = jnp.concatenate([r[24:32], r[24:32]], axis=0)[:, 2 * width :]
        sum_buf[f, me] = jnp.concatenate([n_part, m_part], axis=1).astype(BF16)
        sum_copies[f] = [
            pltpu.make_async_remote_copy(
                src_ref=sum_buf.at[f, me],
                dst_ref=sum_buf.at[f, me],
                send_sem=sum_send.at[f, step],
                recv_sem=sum_recv.at[f, step],
                device_id={"dp": lax.rem(me + step, n_dp)},
                device_id_type=MESH,
            )
            for step in range(1, n_dp)
        ]
        for copy in sum_copies[f]:
            copy.start()
        cond_copies[f] = [
            cond_copy(f, snd_buf.at[f, block_rows(block)], slot, peer)
            for slot, (peer, block) in enumerate(routes)
        ]
        if n_dp == 4:
            for copy, (_, block) in zip(cond_copies[f], routes):
                cond_part(f, both, block)
                copy.start()
            cond_part(f, both, far)
            cond_part(f, both, me)
        else:
            snd_buf[f] = dot(mel[...], both, ((1,), (1,))).astype(BF16)
            for copy in cond_copies[f]:
                copy.start()
        pending += sum_copies[f] + cond_copies[f]
        if f > 0:
            grad_mixed = chan_finish(chan_buf.at[NFLOW + f - 1], copies)
            inner = jnp.concatenate([grad_state[:H], grad_second * gain], axis=0) + grad_mixed
            grad_state = jnp.where(valid, dot_tn(mixes[f], inner), 0.0)

    fin_copies = [None] * NFLOW

    def weight_sums(f):
        for copy in sum_copies[f]:
            copy.wait_recv()
        total = sum_buf[f, 0].astype(F32)
        for block in range(1, n_dp):
            total = total + sum_buf[f, block].astype(F32)
        start_part = jnp.zeros((H, res_size), F32)
        n_rows = cat_rows(total[:, : 2 * width])
        for tap in range(3):
            block = columns(
                lambda c: w_in[f, :, :, c].reshape(2 * width, c.size if isinstance(c, pl.Slice) else res),
                tap * res,
                me * res_size,
                res_size,
                res,
            )
            r = fold_rows(dot(n_rows, block, ((1,), (0,))))
            start_part = start_part + r[tap * H : tap * H + H]
        block = columns(lambda c: w_skip[f, :, c], 0, me * res_size, res_size, res)
        rows = cat_rows(total[0:8, 2 * width :])
        end_part = fold_rows(dot(rows, block, ((1,), (0,))))
        final = jnp.concatenate([start_part, jnp.zeros((8 - H, res_size), F32), end_part], axis=0)
        fin_copies[f] = chan_start(fin_buf.at[f], 2 * NFLOW - 1 + f, final)
        cols = columns_f32(lambda c: basis[f, :, c], me * in_size, in_size, 3 * res)
        o_in[f] = dot_tn(total[:, : 2 * width], cols).reshape(2, width, in_size)
        end_cols = columns_f32(lambda c: w_end_ref[f, :, c], me * res_size, res_size, res)
        o_skip[f] = dot_tn(total[0:8, 2 * width :], end_cols)

    def cond_sums(f):
        total = snd_buf[f, block_rows(me), :].astype(F32)
        for slot, copy in enumerate(cond_copies[f]):
            if n_dp == 4 and slot == 0:
                continue
            copy.wait_recv()
            total = total + rcv_buf[f, slot].astype(F32)
        o_cond[f, 0] = total[: o_cond.shape[2], :width]
        o_cond[f, 1] = total[: o_cond.shape[2], width:]

    cond_relay(1)
    weight_sums(1)
    cond_relay(0)
    weight_sums(0)
    cond_sums(1)
    for f in reversed(range(NFLOW)):
        final = chan_finish(fin_buf.at[f], fin_copies[f])
        o_start[f] = final[:H]
        o_end[f] = final[8:16]
    cond_sums(0)
    for copy in pending:
        copy.wait_send()


def finish(i_start, i_in, i_cond, i_skip, i_end, o_start, o_in, o_cond, o_skip, o_end, sem):
    copies = [
        pltpu.make_async_copy(src, dst, sem.at[at])
        for at, (src, dst) in enumerate(
            [(i_in, o_in), (i_cond, o_cond), (i_skip, o_skip), (i_end, o_end), (i_start, o_start)]
        )
    ]
    for copy in copies:
        copy.start()
    for copy in copies:
        copy.wait()


def on_device(
    audio,
    mel,
    crop_len,
    pack_offset,
    low_mix,
    up_mix,
    log_scale,
    w_start,
    w_in,
    w_cond,
    w_skip,
    w_end,
):
    n_dp = lax.axis_size("dp")
    n_chan = lax.axis_size("chan")
    groups, _, slots = audio.shape
    channels = mel.shape[0]
    _, _, width, taps = w_in.shape
    res = w_end.shape[2]
    audio = audio.reshape(groups, slots)
    mel = mel.reshape(channels, slots)
    rows = channels // n_dp
    padded = -(-rows // 16) * 16
    if padded != rows:
        mel = jnp.pad(mel.reshape(n_dp, rows, slots), ((0, 0), (0, padded - rows), (0, 0)))
        mel = mel.reshape(n_dp * padded, slots)
        w_cond = jnp.pad(
            w_cond.reshape(NFLOW, 2, width, n_dp, rows),
            ((0, 0), (0, 0), (0, 0), (0, 0), (0, padded - rows)),
        ).reshape(NFLOW, 2, width, n_dp * padded)
    vmem = pl.BlockSpec(memory_space=pltpu.VMEM)
    hbm = pl.BlockSpec(memory_space=pltpu.HBM)
    res_size = res // n_dp
    out_shape = (
        jax.ShapeDtypeStruct((NFLOW, H, res_size), F32),
        jax.ShapeDtypeStruct((NFLOW, 2, width, taps // n_dp), F32),
        jax.ShapeDtypeStruct((NFLOW, 2, rows, width), F32),
        jax.ShapeDtypeStruct((NFLOW, width, res_size), F32),
        jax.ShapeDtypeStruct((NFLOW, 2 * H, res_size), F32),
    )
    results = pl.pallas_call(
        functools.partial(kernel, n_dp, n_chan),
        out_shape=out_shape,
        in_specs=[hbm] * 11,
        out_specs=[vmem] * 5,
        scratch_shapes=[
            pltpu.SMEM(crop_len.shape, jnp.int32),
            pltpu.VMEM(audio.shape, BF16),
            pltpu.VMEM(low_mix.shape, F32),
            pltpu.VMEM(up_mix.shape, F32),
            pltpu.VMEM(log_scale.shape, F32),
            pltpu.VMEM(w_start.shape, F32),
            pltpu.VMEM(w_end.shape, F32),
            pltpu.VMEM(mel.shape, BF16),
            pltpu.VMEM(w_in.shape, BF16),
            pltpu.VMEM(w_cond.shape, BF16),
            pltpu.VMEM(w_skip.shape, BF16),
            pltpu.VMEM((NFLOW, 8, res), F32),
            pltpu.VMEM((NFLOW, 16, 3 * res), F32),
            pltpu.VMEM((NFLOW, 2 * width, slots), F32),
            pltpu.VMEM((2 * NFLOW - 1, n_chan, 8, slots), F32),
            pltpu.VMEM((NFLOW, n_chan, 16, res_size), F32),
            pltpu.VMEM((NFLOW, n_dp, 16, 3 * width), BF16),
            pltpu.VMEM((NFLOW, n_dp * padded, 2 * width), BF16),
            pltpu.VMEM((NFLOW, n_dp - 1, padded, 2 * width), BF16),
            pltpu.VMEM((NFLOW, padded, 2 * width), BF16),
            pltpu.SemaphoreType.DMA((13,)),
            pltpu.SemaphoreType.DMA((3 * NFLOW - 1, n_chan)),
            pltpu.SemaphoreType.DMA((3 * NFLOW - 1, n_chan)),
            pltpu.SemaphoreType.DMA((NFLOW, n_dp)),
            pltpu.SemaphoreType.DMA((NFLOW, n_dp)),
            pltpu.SemaphoreType.DMA((NFLOW, n_dp)),
            pltpu.SemaphoreType.DMA((NFLOW, n_dp)),
        ],
        compiler_params=pltpu.CompilerParams(
            collective_id=0, has_side_effects=True, vmem_limit_bytes=24 * 1024 * 1024
        ),
        name="flow_steps",
    )(*[
        pltpu.with_memory_space_constraint(a, pltpu.HBM)
        for a in (
            crop_len, audio, low_mix, up_mix, log_scale, w_start, w_end, mel, w_in, w_cond, w_skip
        )
    ])
    g_start, g_in, g_cond, g_skip, g_end = pl.pallas_call(
        finish,
        out_shape=out_shape,
        in_specs=[vmem] * 5,
        out_specs=[hbm] * 5,
        scratch_shapes=[pltpu.SemaphoreType.DMA((5,))],
        compiler_params=pltpu.CompilerParams(vmem_limit_bytes=16 * 1024 * 1024),
        name="finish",
    )(*results)
    return g_start, g_in, jnp.swapaxes(g_cond, 2, 3), g_skip, g_end


def solution(mesh):
    in_specs = (
        P(None, ("group", "dp"), None),
        P(None, ("group", "dp"), None),
        P("group", None),
        P("group", None),
        P(),
        P(),
        P(),
        P(),
        P(None, None, "chan", None),
        P(None, None, "chan", None),
        P(None, "chan", None),
        P(),
    )
    out_specs = (
        P("group", None, "dp"),
        P("group", None, "chan", "dp"),
        P("group", None, "chan", "dp"),
        P("group", "chan", "dp"),
        P("group", None, "dp"),
    )
    return jax.shard_map(
        on_device, mesh=mesh, in_specs=in_specs, out_specs=out_specs, check_vma=False
    )
```

```python
import functools
import math

import jax
import jax.numpy as jnp
from jax import lax
from jax.experimental import pallas as pl
from jax.experimental.pallas import tpu as pltpu
from jax.sharding import PartitionSpec as P

H = 4
NFLOW = 2
PACK = 256
MESH = pl.DeviceIdType.MESH
F32 = jnp.float32
BF16 = jnp.bfloat16


def dot(a, b, dims):
    return lax.dot_general(a, b, (dims, ((), ())), preferred_element_type=F32)


def halves(a):
    high = a.astype(BF16).astype(F32)
    return high, a - high


def cat_left(a):
    high, low = halves(a)
    return jnp.concatenate([high, high, low], axis=0).astype(BF16)


def cat_right(b):
    high, low = halves(b)
    return jnp.concatenate([high, low, high], axis=0).astype(BF16)


def dot_tn(a, b):
    return dot(cat_left(a), cat_right(b), ((0,), (0,)))


def cat_rows(a):
    high, low = halves(a)
    return jnp.concatenate([high, low], axis=0).astype(BF16)


def fold_rows(r):
    half = r.shape[0] // 2
    return r[:half] + r[half:]


def columns(read, base, start, size, full):
    if size % 128 == 0:
        return read(pl.ds(pl.multiple_of(base + start, 128), size))
    row = lax.broadcasted_iota(jnp.int32, (full, size), 0)
    col = lax.broadcasted_iota(jnp.int32, (full, size), 1)
    pick = jnp.where(row == col + start, 1.0, 0.0).astype(BF16)
    return dot(read(slice(base, base + full)), pick, ((1,), (0,))).astype(BF16)


def columns_f32(read, start, size, full):
    if size % 128 == 0:
        return read(pl.ds(pl.multiple_of(start, 128), size))
    row = lax.broadcasted_iota(jnp.int32, (full, size), 0)
    col = lax.broadcasted_iota(jnp.int32, (full, size), 1)
    pick = jnp.where(row == col + start, 1.0, 0.0).astype(BF16)
    return fold_rows(dot(cat_rows(read(slice(None))), pick, ((1,), (0,))))


def kernel(
    n_dp,
    n_chan,
    len_hbm,
    audio_hbm,
    low_hbm,
    up_hbm,
    scale_hbm,
    w_start_hbm,
    w_end_hbm,
    mel_hbm,
    w_in_hbm,
    w_cond_hbm,
    w_skip_hbm,
    o_start,
    o_in,
    o_cond,
    o_skip,
    o_end,
    len_ref,
    audio_ref,
    low_ref,
    up_ref,
    scale_ref,
    w_start_ref,
    w_end_ref,
    mel,
    w_in,
    w_cond,
    w_skip,
    w_first,
    basis,
    cond,
    chan_buf,
    fin_buf,
    sum_buf,
    snd_buf,
    rcv_buf,
    fwd_buf,
    load_sem,
    chan_send,
    chan_recv,
    sum_send,
    sum_recv,
    cond_send,
    cond_recv,
):
    slots = audio_ref.shape[1]
    cap = slots // n_dp
    width = w_in_hbm.shape[2]
    res = w_end_ref.shape[2]
    mel_rows = mel_hbm.shape[0] // n_dp
    res_size = o_skip.shape[2]
    in_size = o_in.shape[3]
    obj_scale = 8.0 / math.sqrt(n_dp * PACK)
    me = lax.axis_index("dp")
    chan = lax.axis_index("chan")

    barrier = pltpu.get_barrier_semaphore()
    for step in range(1, n_chan):
        peer = lax.rem(chan + step, n_chan)
        pl.semaphore_signal(barrier, inc=1, device_id={"chan": peer}, device_id_type=MESH)
    for step in range(1, n_dp):
        peer = lax.rem(me + step, n_dp)
        pl.semaphore_signal(barrier, inc=1, device_id={"dp": peer}, device_id_type=MESH)

    pairs = {
        "start": (w_start_hbm, w_start_ref),
        "in0": (w_in_hbm.at[0], w_in.at[0]),
        "len": (len_hbm, len_ref),
        "audio": (audio_hbm, audio_ref),
        "low": (low_hbm, low_ref),
        "up": (up_hbm, up_ref),
        "scale": (scale_hbm, scale_ref),
        "end": (w_end_hbm, w_end_ref),
        "skip": (w_skip_hbm, w_skip),
        "mel": (mel_hbm, mel),
        "cond0": (w_cond_hbm.at[0], w_cond.at[0]),
        "in1": (w_in_hbm.at[1], w_in.at[1]),
        "cond1": (w_cond_hbm.at[1], w_cond.at[1]),
    }
    loads = {
        key: pltpu.make_async_copy(src, dst, load_sem.at[at])
        for at, (key, (src, dst)) in enumerate(pairs.items())
    }
    for load in loads.values():
        load.start()

    def chan_start(buf, phase, value):
        buf[chan] = value
        copies = [
            pltpu.make_async_remote_copy(
                src_ref=buf.at[chan],
                dst_ref=buf.at[chan],
                send_sem=chan_send.at[phase, step],
                recv_sem=chan_recv.at[phase, step],
                device_id={"chan": lax.rem(chan + step, n_chan)},
                device_id_type=MESH,
            )
            for step in range(1, n_chan)
        ]
        for copy in copies:
            copy.start()
        pending.extend(copies)
        return copies

    def chan_finish(buf, copies):
        for copy in copies:
            copy.wait_recv()
        total = buf[0]
        for block in range(1, n_chan):
            total = total + buf[block]
        return total

    pending = []
    w_first[...] = jnp.zeros(w_first.shape, F32)
    basis[...] = jnp.zeros(basis.shape, F32)

    for key in ("len", "audio", "low", "up", "scale"):
        loads[key].wait()
    column = lax.broadcasted_iota(jnp.int32, (8, slots), 1)
    owner = column // cap
    within = column - owner * cap
    lens = jnp.zeros((8, slots), jnp.int32)
    for block in range(n_dp):
        lens = jnp.where(owner == block, len_ref[block, me], lens)
    valid = within < lens
    prev_mask = valid & (within >= 1)
    next_mask = within + 1 < lens

    row8 = lax.broadcasted_iota(jnp.int32, (8, 8), 0)
    col8 = lax.broadcasted_iota(jnp.int32, (8, 8), 1)
    mixes = []
    for f in range(NFLOW):
        lower = jnp.where(row8 > col8, low_ref[f], jnp.where(row8 == col8, 1.0, 0.0))
        diag = jnp.broadcast_to(jnp.exp(scale_ref[f : f + 1, :]), (8, 8))
        upper = jnp.where(row8 < col8, up_ref[f], jnp.where(row8 == col8, diag, 0.0))
        mixing = lower[:, 0:1] * upper[0:1, :]
        for k in range(1, 8):
            mixing = mixing + lower[:, k : k + 1] * upper[k : k + 1, :]
        mixes.append(mixing)

    def mix(f, x):
        mixing = mixes[f]
        mixed = mixing[:, 0:1] * x[0:1, :]
        for k in range(1, 8):
            mixed = mixed + mixing[:, k : k + 1] * x[k : k + 1, :]
        return mixed

    w_eff = [None] * NFLOW
    b_skip = [None] * NFLOW

    def precompute(f):
        loads["in%d" % f].wait()
        start16 = cat_rows(w_first[f])
        taps = []
        for tap in range(3):
            block = w_in[f, :, :, tap * res : (tap + 1) * res].reshape(2 * width, res)
            taps.append(fold_rows(dot(start16, block, ((1,), (1,)))))
        w_eff[f] = jnp.concatenate(taps, axis=0)
        if f == 0:
            loads["end"].wait()
            loads["skip"].wait()
        b_skip[f] = fold_rows(dot(cat_rows(w_end_ref[f]), w_skip[f], ((1,), (1,))))
        if f == 0:
            loads["mel"].wait()
        loads["cond%d" % f].wait()
        every = w_cond[f].reshape(2 * width, w_cond.shape[3])
        cond[f] = dot(every, mel[...], ((1,), (0,)))

    x_state = jnp.where(valid, audio_ref[...].astype(F32), 0.0)
    loads["start"].wait()
    for f in range(NFLOW):
        w_first[f, :H] = w_start_ref[f]
    precompute(0)
    saved = []
    for f in range(NFLOW):
        mixed = mix(f, x_state)
        stacked = jnp.concatenate(
            [
                jnp.where(prev_mask, pltpu.roll(mixed, 1, 1), 0.0),
                mixed,
                jnp.where(next_mask, pltpu.roll(mixed, slots - 1, 1), 0.0),
            ],
            axis=0,
        )
        pre = dot_tn(w_eff[f], stacked) + cond[f]
        tanh_val = jnp.tanh(pre[:width])
        sigm_val = 0.5 * jnp.tanh(0.5 * pre[width:]) + 0.5
        gated = (tanh_val * sigm_val).astype(BF16)
        part = fold_rows(dot(cat_rows(b_skip[f]), gated, ((1,), (0,))))
        if f == 0:
            pl.semaphore_wait(barrier, n_chan + n_dp - 2)
        copies = chan_start(chan_buf.at[f], f, part)
        if f == 0:
            precompute(1)
            for g in range(NFLOW):
                for tap in range(3):
                    basis[g, tap * H : tap * H + H, tap * res : (tap + 1) * res] = w_start_ref[g]
        slope_tanh = sigm_val * (1.0 - tanh_val * tanh_val)
        slope_sigm = tanh_val * sigm_val * (1.0 - sigm_val)
        coupling = chan_finish(chan_buf.at[f], copies)
        gain = jnp.exp(coupling[:H])
        second = mixed[H:]
        saved.append((mixed, stacked, slope_tanh, slope_sigm, gated, gain))
        x_state = jnp.where(
            valid, jnp.concatenate([mixed[:H], gain * second + coupling[H:]], axis=0), 0.0
        )

    side = me + 1 - 2 * lax.rem(me, 2)
    far = lax.rem(me + 2, n_dp)
    diag = lax.rem(side + 2, n_dp)
    half = mel_rows // 32 * 16
    top, low_rows = (0, half), (half, mel_rows - half)
    whole = (0, mel_rows)

    def block_rows(block, part=whole):
        start, size = part
        return pl.ds(pl.multiple_of(block * mel_rows + start, 16), size)

    def cond_start(f, source, slot, part, peer, at):
        copy = pltpu.make_async_remote_copy(
            src_ref=source,
            dst_ref=rcv_buf.at[f, slot, pl.ds(*part)],
            send_sem=cond_send.at[f, at],
            recv_sem=cond_recv.at[f, at],
            device_id={"dp": peer},
            device_id_type=MESH,
        )
        copy.start()
        pending.append(copy)
        cond_copies[f][at] = copy

    def cond_send_block(f, block, slot, part, peer, at):
        cond_start(f, snd_buf.at[f, block_rows(block, part)], slot, part, peer, at)

    def cond_part(f, both, block):
        rows = block_rows(block)
        snd_buf[f, rows, :] = dot(mel[rows, :], both, ((1,), (1,))).astype(BF16)

    def cond_relay(f):
        if n_dp != 4:
            return
        cond_copies[f][0].wait_recv()
        total = snd_buf[f, block_rows(far, top), :].astype(F32) + rcv_buf[f, 0, pl.ds(*top)].astype(F32)
        fwd_buf[f] = total.astype(BF16)
        cond_start(f, fwd_buf.at[f], 2, top, far, 2)

    grad_state = obj_scale * x_state
    sum_copies = [None] * NFLOW
    cond_copies = [{} for _ in range(NFLOW)]
    for f in reversed(range(NFLOW)):
        mixed, stacked, slope_tanh, slope_sigm, gated, gain = saved[f]
        grad_second = grad_state[H:]
        grad_log = grad_second * gain * mixed[H:] - obj_scale
        grad_coupling = jnp.where(
            valid, jnp.concatenate([grad_log, grad_second], axis=0), 0.0
        )
        grad_gated = dot_tn(b_skip[f], grad_coupling)
        grad_tanh = (grad_gated * slope_tanh).astype(BF16)
        grad_sigm = (grad_gated * slope_sigm).astype(BF16)
        both = jnp.concatenate([grad_tanh, grad_sigm], axis=0)
        if f > 0:
            back = fold_rows(dot(cat_rows(w_eff[f]), both, ((1,), (0,))))
            part = (
                back[8:16]
                + pltpu.roll(jnp.where(prev_mask, back[0:8], 0.0), slots - 1, 1)
                + pltpu.roll(jnp.where(next_mask, back[16:24], 0.0), 1, 1)
            )
            copies = chan_start(chan_buf.at[NFLOW + f - 1], NFLOW + f - 1, part)
        if n_dp == 4:
            cond_part(f, both, diag)
            cond_send_block(f, diag, 0, top, side, 0)
            cond_send_block(f, diag, 3, low_rows, diag, 4)
        left = cat_rows(jnp.concatenate([stacked, grad_coupling], axis=0))
        values = jnp.concatenate([both, gated], axis=0)
        r = fold_rows(dot(left, values, ((1,), (1,))))
        n_part = jnp.concatenate([r[0:4], r[8:12], r[16:20], r[20:24]], axis=0)[:, : 2 * width]
        m_part = jnp.concatenate([r[24:32], r[24:32]], axis=0)[:, 2 * width :]
        sum_buf[f, me] = jnp.concatenate([n_part, m_part], axis=1).astype(BF16)
        sum_copies[f] = [
            pltpu.make_async_remote_copy(
                src_ref=sum_buf.at[f, me],
                dst_ref=sum_buf.at[f, me],
                send_sem=sum_send.at[f, step],
                recv_sem=sum_recv.at[f, step],
                device_id={"dp": lax.rem(me + step, n_dp)},
                device_id_type=MESH,
            )
            for step in range(1, n_dp)
        ]
        for copy in sum_copies[f]:
            copy.start()
        pending += sum_copies[f]
        if n_dp == 4:
            cond_part(f, both, far)
            cond_send_block(f, far, 2, low_rows, far, 3)
            cond_part(f, both, side)
            cond_send_block(f, side, 1, whole, side, 1)
            cond_part(f, both, me)
        else:
            snd_buf[f] = dot(mel[...], both, ((1,), (1,))).astype(BF16)
            for step in range(1, n_dp):
                peer = lax.rem(me + step, n_dp)
                cond_send_block(f, peer, step - 1, whole, peer, step - 1)
        if f > 0:
            grad_mixed = chan_finish(chan_buf.at[NFLOW + f - 1], copies)
            inner = jnp.concatenate([grad_state[:H], grad_second * gain], axis=0) + grad_mixed
            grad_state = jnp.where(valid, dot_tn(mixes[f], inner), 0.0)

    fin_copies = [None] * NFLOW

    def weight_sums(f):
        for copy in sum_copies[f]:
            copy.wait_recv()
        total = sum_buf[f, 0].astype(F32)
        for block in range(1, n_dp):
            total = total + sum_buf[f, block].astype(F32)
        start_part = jnp.zeros((H, res_size), F32)
        n_rows = cat_rows(total[:, : 2 * width])
        for tap in range(3):
            block = columns(
                lambda c: w_in[f, :, :, c].reshape(2 * width, c.size if isinstance(c, pl.Slice) else res),
                tap * res,
                me * res_size,
                res_size,
                res,
            )
            r = fold_rows(dot(n_rows, block, ((1,), (0,))))
            start_part = start_part + r[tap * H : tap * H + H]
        block = columns(lambda c: w_skip[f, :, c], 0, me * res_size, res_size, res)
        rows = cat_rows(total[0:8, 2 * width :])
        end_part = fold_rows(dot(rows, block, ((1,), (0,))))
        final = jnp.concatenate([start_part, jnp.zeros((8 - H, res_size), F32), end_part], axis=0)
        fin_copies[f] = chan_start(fin_buf.at[f], 2 * NFLOW - 1 + f, final)
        cols = columns_f32(lambda c: basis[f, :, c], me * in_size, in_size, 3 * res)
        o_in[f] = dot_tn(total[:, : 2 * width], cols).reshape(2, width, in_size)
        end_cols = columns_f32(lambda c: w_end_ref[f, :, c], me * res_size, res_size, res)
        o_skip[f] = dot_tn(total[0:8, 2 * width :], end_cols)

    def cond_sums(f):
        if n_dp == 4:
            pieces = [(low_rows, {1: 1, 3: 2, 4: 3}), (top, {1: 1, 2: 2})]
        else:
            pieces = [(whole, {at: at for at in range(n_dp - 1)})]
        waited = set()
        for part, slots_of in pieces:
            total = snd_buf[f, block_rows(me, part), :].astype(F32)
            for at, slot in slots_of.items():
                if at not in waited:
                    cond_copies[f][at].wait_recv()
                    waited.add(at)
                total = total + rcv_buf[f, slot, pl.ds(*part)].astype(F32)
            start = part[0]
            rows = min(part[1], o_cond.shape[2] - start)
            o_cond[f, 0, start : start + rows] = total[:rows, :width]
            o_cond[f, 1, start : start + rows] = total[:rows, width:]

    cond_relay(1)
    weight_sums(1)
    cond_relay(0)
    weight_sums(0)
    cond_sums(1)
    for f in reversed(range(NFLOW)):
        final = chan_finish(fin_buf.at[f], fin_copies[f])
        o_start[f] = final[:H]
        o_end[f] = final[8:16]
    cond_sums(0)
    for copy in pending:
        copy.wait_send()


def finish(i_start, i_in, i_cond, i_skip, i_end, o_start, o_in, o_cond, o_skip, o_end, sem):
    copies = [
        pltpu.make_async_copy(src, dst, sem.at[at])
        for at, (src, dst) in enumerate(
            [(i_in, o_in), (i_cond, o_cond), (i_skip, o_skip), (i_end, o_end), (i_start, o_start)]
        )
    ]
    for copy in copies:
        copy.start()
    for copy in copies:
        copy.wait()


def on_device(
    audio,
    mel,
    crop_len,
    pack_offset,
    low_mix,
    up_mix,
    log_scale,
    w_start,
    w_in,
    w_cond,
    w_skip,
    w_end,
):
    n_dp = lax.axis_size("dp")
    n_chan = lax.axis_size("chan")
    groups, _, slots = audio.shape
    channels = mel.shape[0]
    _, _, width, taps = w_in.shape
    res = w_end.shape[2]
    audio = audio.reshape(groups, slots)
    mel = mel.reshape(channels, slots)
    rows = channels // n_dp
    padded = -(-rows // 16) * 16
    if padded != rows:
        mel = jnp.pad(mel.reshape(n_dp, rows, slots), ((0, 0), (0, padded - rows), (0, 0)))
        mel = mel.reshape(n_dp * padded, slots)
        w_cond = jnp.pad(
            w_cond.reshape(NFLOW, 2, width, n_dp, rows),
            ((0, 0), (0, 0), (0, 0), (0, 0), (0, padded - rows)),
        ).reshape(NFLOW, 2, width, n_dp * padded)
    vmem = pl.BlockSpec(memory_space=pltpu.VMEM)
    hbm = pl.BlockSpec(memory_space=pltpu.HBM)
    res_size = res // n_dp
    out_shape = (
        jax.ShapeDtypeStruct((NFLOW, H, res_size), F32),
        jax.ShapeDtypeStruct((NFLOW, 2, width, taps // n_dp), F32),
        jax.ShapeDtypeStruct((NFLOW, 2, rows, width), F32),
        jax.ShapeDtypeStruct((NFLOW, width, res_size), F32),
        jax.ShapeDtypeStruct((NFLOW, 2 * H, res_size), F32),
    )
    results = pl.pallas_call(
        functools.partial(kernel, n_dp, n_chan),
        out_shape=out_shape,
        in_specs=[hbm] * 11,
        out_specs=[vmem] * 5,
        scratch_shapes=[
            pltpu.SMEM(crop_len.shape, jnp.int32),
            pltpu.VMEM(audio.shape, BF16),
            pltpu.VMEM(low_mix.shape, F32),
            pltpu.VMEM(up_mix.shape, F32),
            pltpu.VMEM(log_scale.shape, F32),
            pltpu.VMEM(w_start.shape, F32),
            pltpu.VMEM(w_end.shape, F32),
            pltpu.VMEM(mel.shape, BF16),
            pltpu.VMEM(w_in.shape, BF16),
            pltpu.VMEM(w_cond.shape, BF16),
            pltpu.VMEM(w_skip.shape, BF16),
            pltpu.VMEM((NFLOW, 8, res), F32),
            pltpu.VMEM((NFLOW, 16, 3 * res), F32),
            pltpu.VMEM((NFLOW, 2 * width, slots), F32),
            pltpu.VMEM((2 * NFLOW - 1, n_chan, 8, slots), F32),
            pltpu.VMEM((NFLOW, n_chan, 16, res_size), F32),
            pltpu.VMEM((NFLOW, n_dp, 16, 3 * width), BF16),
            pltpu.VMEM((NFLOW, n_dp * padded, 2 * width), BF16),
            pltpu.VMEM((NFLOW, max(n_dp - 1, 4), padded, 2 * width), BF16),
            pltpu.VMEM((NFLOW, max(padded // 32, 1) * 16, 2 * width), BF16),
            pltpu.SemaphoreType.DMA((13,)),
            pltpu.SemaphoreType.DMA((3 * NFLOW - 1, n_chan)),
            pltpu.SemaphoreType.DMA((3 * NFLOW - 1, n_chan)),
            pltpu.SemaphoreType.DMA((NFLOW, n_dp)),
            pltpu.SemaphoreType.DMA((NFLOW, n_dp)),
            pltpu.SemaphoreType.DMA((NFLOW, max(n_dp, 5))),
            pltpu.SemaphoreType.DMA((NFLOW, max(n_dp, 5))),
        ],
        compiler_params=pltpu.CompilerParams(
            collective_id=0, has_side_effects=True, vmem_limit_bytes=24 * 1024 * 1024
        ),
        name="flow_steps",
    )(*[
        pltpu.with_memory_space_constraint(a, pltpu.HBM)
        for a in (
            crop_len, audio, low_mix, up_mix, log_scale, w_start, w_end, mel, w_in, w_cond, w_skip
        )
    ])
    g_start, g_in, g_cond, g_skip, g_end = pl.pallas_call(
        finish,
        out_shape=out_shape,
        in_specs=[vmem] * 5,
        out_specs=[hbm] * 5,
        scratch_shapes=[pltpu.SemaphoreType.DMA((5,))],
        compiler_params=pltpu.CompilerParams(vmem_limit_bytes=16 * 1024 * 1024),
        name="finish",
    )(*results)
    return g_start, g_in, jnp.swapaxes(g_cond, 2, 3), g_skip, g_end


def solution(mesh):
    in_specs = (
        P(None, ("group", "dp"), None),
        P(None, ("group", "dp"), None),
        P("group", None),
        P("group", None),
        P(),
        P(),
        P(),
        P(),
        P(None, None, "chan", None),
        P(None, None, "chan", None),
        P(None, "chan", None),
        P(),
    )
    out_specs = (
        P("group", None, "dp"),
        P("group", None, "chan", "dp"),
        P("group", None, "chan", "dp"),
        P("group", "chan", "dp"),
        P("group", None, "dp"),
    )
    return jax.shard_map(
        on_device, mesh=mesh, in_specs=in_specs, out_specs=out_specs, check_vma=False
    )
```

```python
import functools
import math

import jax
import jax.numpy as jnp
from jax import lax
from jax.experimental import pallas as pl
from jax.experimental.pallas import tpu as pltpu
from jax.sharding import PartitionSpec as P

H = 4
NFLOW = 2
PACK = 256
MESH = pl.DeviceIdType.MESH
F32 = jnp.float32
BF16 = jnp.bfloat16


def dot(a, b, dims):
    return lax.dot_general(a, b, (dims, ((), ())), preferred_element_type=F32)


def halves(a):
    high = a.astype(BF16).astype(F32)
    return high, a - high


def cat_left(a):
    high, low = halves(a)
    return jnp.concatenate([high, high, low], axis=0).astype(BF16)


def cat_right(b):
    high, low = halves(b)
    return jnp.concatenate([high, low, high], axis=0).astype(BF16)


def dot_tn(a, b):
    return dot(cat_left(a), cat_right(b), ((0,), (0,)))


def cat_rows(a):
    high, low = halves(a)
    return jnp.concatenate([high, low], axis=0).astype(BF16)


def fold_rows(r):
    half = r.shape[0] // 2
    return r[:half] + r[half:]


def columns(read, base, start, size, full):
    if size % 128 == 0:
        return read(pl.ds(pl.multiple_of(base + start, 128), size))
    row = lax.broadcasted_iota(jnp.int32, (full, size), 0)
    col = lax.broadcasted_iota(jnp.int32, (full, size), 1)
    pick = jnp.where(row == col + start, 1.0, 0.0).astype(BF16)
    return dot(read(slice(base, base + full)), pick, ((1,), (0,))).astype(BF16)


def columns_f32(read, start, size, full):
    if size % 128 == 0:
        return read(pl.ds(pl.multiple_of(start, 128), size))
    row = lax.broadcasted_iota(jnp.int32, (full, size), 0)
    col = lax.broadcasted_iota(jnp.int32, (full, size), 1)
    pick = jnp.where(row == col + start, 1.0, 0.0).astype(BF16)
    return fold_rows(dot(cat_rows(read(slice(None))), pick, ((1,), (0,))))


def kernel(
    n_dp,
    n_chan,
    len_hbm,
    audio_hbm,
    low_hbm,
    up_hbm,
    scale_hbm,
    w_start_hbm,
    w_end_hbm,
    mel_hbm,
    w_in_hbm,
    w_cond_hbm,
    w_skip_hbm,
    o_start,
    o_in,
    o_cond,
    o_skip,
    o_end,
    len_ref,
    audio_ref,
    low_ref,
    up_ref,
    scale_ref,
    w_start_ref,
    w_end_ref,
    mel,
    w_in,
    w_cond,
    w_skip,
    w_first,
    basis,
    cond,
    chan_buf,
    fin_buf,
    sum_buf,
    snd_buf,
    rcv_buf,
    fwd_buf,
    load_sem,
    chan_send,
    chan_recv,
    sum_send,
    sum_recv,
    cond_send,
    cond_recv,
    go,
):
    slots = audio_ref.shape[1]
    cap = slots // n_dp
    width = w_in_hbm.shape[2]
    res = w_end_ref.shape[2]
    mel_rows = mel_hbm.shape[0] // n_dp
    res_size = o_skip.shape[2]
    in_size = o_in.shape[3]
    obj_scale = 8.0 / math.sqrt(n_dp * PACK)
    me = lax.axis_index("dp")
    chan = lax.axis_index("chan")

    barrier = pltpu.get_barrier_semaphore()
    split = n_chan == 4
    core = lax.rem(chan, 2)
    even, odd = chan - core, chan - core + 1

    def signal(semaphore, **device):
        pl.semaphore_signal(semaphore, inc=1, device_id=device, device_id_type=MESH)

    if split:
        signal(barrier, chan=lax.rem(even + 2, n_chan))

        @pl.when(core == 1)
        def _():
            signal(barrier, chan=even)
    else:
        for step in range(1, n_chan):
            signal(barrier, chan=lax.rem(chan + step, n_chan))
        for step in range(1, n_dp):
            signal(barrier, dp=lax.rem(me + step, n_dp))

    def chan_ready():
        if not split:
            pl.semaphore_wait(barrier, n_chan + n_dp - 2)
            return

        @pl.when(core == 0)
        def _():
            pl.semaphore_wait(barrier, n_chan - 1)
            signal(go.at[0], chan=odd)

        @pl.when(core == 1)
        def _():
            pl.semaphore_wait(go.at[0], 1)

    def dp_ready():
        if not split:
            return

        @pl.when(core == 1)
        def _():
            pl.semaphore_wait(barrier, 2 * (n_dp - 1))
            signal(go.at[1], chan=even)

        @pl.when(core == 0)
        def _():
            pl.semaphore_wait(go.at[1], 1)

    pairs = {
        "start": (w_start_hbm, w_start_ref),
        "in0": (w_in_hbm.at[0], w_in.at[0]),
        "len": (len_hbm, len_ref),
        "audio": (audio_hbm, audio_ref),
        "low": (low_hbm, low_ref),
        "up": (up_hbm, up_ref),
        "scale": (scale_hbm, scale_ref),
        "end": (w_end_hbm, w_end_ref),
        "skip": (w_skip_hbm, w_skip),
        "mel": (mel_hbm, mel),
        "cond0": (w_cond_hbm.at[0], w_cond.at[0]),
        "in1": (w_in_hbm.at[1], w_in.at[1]),
        "cond1": (w_cond_hbm.at[1], w_cond.at[1]),
    }
    loads = {
        key: pltpu.make_async_copy(src, dst, load_sem.at[at])
        for at, (key, (src, dst)) in enumerate(pairs.items())
    }
    for load in loads.values():
        load.start()
    if split:
        for step in range(1, n_dp):
            signal(barrier, dp=lax.rem(me + step, n_dp), chan=odd)

    def chan_start(buf, phase, value):
        buf[chan] = value
        copies = [
            pltpu.make_async_remote_copy(
                src_ref=buf.at[chan],
                dst_ref=buf.at[chan],
                send_sem=chan_send.at[phase, step],
                recv_sem=chan_recv.at[phase, step],
                device_id={"chan": lax.rem(chan + step, n_chan)},
                device_id_type=MESH,
            )
            for step in sorted(range(1, n_chan), key=lambda step: abs(2 * step - n_chan))
        ]
        for copy in copies:
            copy.start()
        pending.extend(copies)
        return copies

    def chan_finish(buf, copies):
        for copy in copies:
            copy.wait_recv()
        total = buf[0]
        for block in range(1, n_chan):
            total = total + buf[block]
        return total

    pending = []
    w_first[...] = jnp.zeros(w_first.shape, F32)
    basis[...] = jnp.zeros(basis.shape, F32)

    for key in ("len", "audio", "low", "up", "scale"):
        loads[key].wait()
    column = lax.broadcasted_iota(jnp.int32, (8, slots), 1)
    owner = column // cap
    within = column - owner * cap
    lens = jnp.zeros((8, slots), jnp.int32)
    for block in range(n_dp):
        lens = jnp.where(owner == block, len_ref[block, me], lens)
    valid = within < lens
    prev_mask = valid & (within >= 1)
    next_mask = within + 1 < lens

    row8 = lax.broadcasted_iota(jnp.int32, (8, 8), 0)
    col8 = lax.broadcasted_iota(jnp.int32, (8, 8), 1)
    mixes = []
    for f in range(NFLOW):
        lower = jnp.where(row8 > col8, low_ref[f], jnp.where(row8 == col8, 1.0, 0.0))
        diag = jnp.broadcast_to(jnp.exp(scale_ref[f : f + 1, :]), (8, 8))
        upper = jnp.where(row8 < col8, up_ref[f], jnp.where(row8 == col8, diag, 0.0))
        mixing = lower[:, 0:1] * upper[0:1, :]
        for k in range(1, 8):
            mixing = mixing + lower[:, k : k + 1] * upper[k : k + 1, :]
        mixes.append(mixing)

    def mix(f, x):
        mixing = mixes[f]
        mixed = mixing[:, 0:1] * x[0:1, :]
        for k in range(1, 8):
            mixed = mixed + mixing[:, k : k + 1] * x[k : k + 1, :]
        return mixed

    w_eff = [None] * NFLOW
    b_skip = [None] * NFLOW

    def precompute(f):
        loads["in%d" % f].wait()
        start16 = cat_rows(w_first[f])
        taps = []
        for tap in range(3):
            block = w_in[f, :, :, tap * res : (tap + 1) * res].reshape(2 * width, res)
            taps.append(fold_rows(dot(start16, block, ((1,), (1,)))))
        w_eff[f] = jnp.concatenate(taps, axis=0)
        if f == 0:
            loads["end"].wait()
            loads["skip"].wait()
        b_skip[f] = fold_rows(dot(cat_rows(w_end_ref[f]), w_skip[f], ((1,), (1,))))
        if f == 0:
            loads["mel"].wait()
        loads["cond%d" % f].wait()
        every = w_cond[f].reshape(2 * width, w_cond.shape[3])
        cond[f] = dot(every, mel[...], ((1,), (0,)))

    x_state = jnp.where(valid, audio_ref[...].astype(F32), 0.0)
    loads["start"].wait()
    for f in range(NFLOW):
        w_first[f, :H] = w_start_ref[f]
    precompute(0)
    saved = []
    for f in range(NFLOW):
        mixed = mix(f, x_state)
        stacked = jnp.concatenate(
            [
                jnp.where(prev_mask, pltpu.roll(mixed, 1, 1), 0.0),
                mixed,
                jnp.where(next_mask, pltpu.roll(mixed, slots - 1, 1), 0.0),
            ],
            axis=0,
        )
        pre = dot_tn(w_eff[f], stacked) + cond[f]
        tanh_val = jnp.tanh(pre[:width])
        sigm_val = 0.5 * jnp.tanh(0.5 * pre[width:]) + 0.5
        gated = (tanh_val * sigm_val).astype(BF16)
        part = fold_rows(dot(cat_rows(b_skip[f]), gated, ((1,), (0,))))
        if f == 0:
            chan_ready()
        copies = chan_start(chan_buf.at[f], f, part)
        if f == 0:
            precompute(1)
            for g in range(NFLOW):
                for tap in range(3):
                    basis[g, tap * H : tap * H + H, tap * res : (tap + 1) * res] = w_start_ref[g]
        slope_tanh = sigm_val * (1.0 - tanh_val * tanh_val)
        slope_sigm = tanh_val * sigm_val * (1.0 - sigm_val)
        coupling = chan_finish(chan_buf.at[f], copies)
        gain = jnp.exp(coupling[:H])
        second = mixed[H:]
        saved.append((mixed, stacked, slope_tanh, slope_sigm, gated, gain))
        x_state = jnp.where(
            valid, jnp.concatenate([mixed[:H], gain * second + coupling[H:]], axis=0), 0.0
        )

    side = me + 1 - 2 * lax.rem(me, 2)
    far = lax.rem(me + 2, n_dp)
    diag = lax.rem(side + 2, n_dp)
    tops = [(0, mel_rows * 64 // 160 // 16 * 16), (0, mel_rows * 80 // 160 // 16 * 16)]
    lows = [(size, mel_rows - size) for _, size in tops]
    whole = (0, mel_rows)

    def block_rows(block, part=whole):
        start, size = part
        return pl.ds(pl.multiple_of(block * mel_rows + start, 16), size)

    def cond_start(f, source, slot, part, peer, at):
        copy = pltpu.make_async_remote_copy(
            src_ref=source,
            dst_ref=rcv_buf.at[f, slot, pl.ds(*part)],
            send_sem=cond_send.at[f, at],
            recv_sem=cond_recv.at[f, at],
            device_id={"dp": peer},
            device_id_type=MESH,
        )
        copy.start()
        pending.append(copy)
        cond_copies[f][at] = copy

    def cond_send_block(f, block, slot, part, peer, at):
        cond_start(f, snd_buf.at[f, block_rows(block, part)], slot, part, peer, at)

    def cond_part(f, both, block):
        rows = block_rows(block)
        snd_buf[f, rows, :] = dot(mel[rows, :], both, ((1,), (1,))).astype(BF16)

    def sum_copy(f, source, slot, peer, at):
        copy = pltpu.make_async_remote_copy(
            src_ref=source,
            dst_ref=sum_buf.at[f, slot],
            send_sem=sum_send.at[f, at],
            recv_sem=sum_recv.at[f, at],
            device_id={"dp": peer},
            device_id_type=MESH,
        )
        copy.start()
        return copy

    def sum_relay(f):
        if n_dp != 4:
            return
        sum_copies[f][0].wait_recv()
        pair = sum_buf[f, me].astype(F32) + sum_buf[f, side].astype(F32)
        sum_buf[f, far] = pair.astype(BF16)
        copy = sum_copy(f, sum_buf.at[f, far], diag, far, 1)
        sum_copies[f].append(copy)
        pending.append(copy)

    def cond_relay(f):
        if n_dp != 4:
            return
        top = tops[f]
        cond_copies[f][0].wait_recv()
        total = snd_buf[f, block_rows(far, top), :].astype(F32) + rcv_buf[f, 0, pl.ds(*top)].astype(F32)
        fwd_buf[f, pl.ds(*top)] = total.astype(BF16)
        cond_start(f, fwd_buf.at[f, pl.ds(*top)], 2, top, far, 2)

    grad_state = obj_scale * x_state
    sum_copies = [None] * NFLOW
    cond_copies = [{} for _ in range(NFLOW)]
    for f in reversed(range(NFLOW)):
        mixed, stacked, slope_tanh, slope_sigm, gated, gain = saved[f]
        grad_second = grad_state[H:]
        grad_log = grad_second * gain * mixed[H:] - obj_scale
        grad_coupling = jnp.where(
            valid, jnp.concatenate([grad_log, grad_second], axis=0), 0.0
        )
        grad_gated = dot_tn(b_skip[f], grad_coupling)
        grad_tanh = (grad_gated * slope_tanh).astype(BF16)
        grad_sigm = (grad_gated * slope_sigm).astype(BF16)
        both = jnp.concatenate([grad_tanh, grad_sigm], axis=0)
        if f > 0:
            back = fold_rows(dot(cat_rows(w_eff[f]), both, ((1,), (0,))))
            part = (
                back[8:16]
                + pltpu.roll(jnp.where(prev_mask, back[0:8], 0.0), slots - 1, 1)
                + pltpu.roll(jnp.where(next_mask, back[16:24], 0.0), 1, 1)
            )
            copies = chan_start(chan_buf.at[NFLOW + f - 1], NFLOW + f - 1, part)
        left = cat_rows(jnp.concatenate([stacked, grad_coupling], axis=0))
        values = jnp.concatenate([both, gated], axis=0)
        r = fold_rows(dot(left, values, ((1,), (1,))))
        n_part = jnp.concatenate([r[0:4], r[8:12], r[16:20]], axis=0)[:, : 2 * width]
        m_part = jnp.concatenate([r[24:28, 2 * width :], r[28:32, 2 * width :]], axis=1)
        sum_buf[f, me] = jnp.concatenate([n_part, m_part], axis=0).astype(BF16)
        if f == NFLOW - 1:
            dp_ready()
        relay = False
        sum_copies[f] = [
            sum_copy(f, sum_buf.at[f, me], me, peer, at)
            for at, peer in enumerate(
                [side] if relay else [lax.rem(me + step, n_dp) for step in range(1, n_dp)]
            )
        ]
        pending += sum_copies[f]
        if n_dp == 4:
            cond_part(f, both, diag)
            cond_send_block(f, diag, 0, tops[f], side, 0)
            cond_send_block(f, diag, 3, lows[f], diag, 4)
        if n_dp == 4:
            cond_part(f, both, far)
            cond_send_block(f, far, 2, lows[f], far, 3)
            cond_part(f, both, side)
            cond_send_block(f, side, 1, whole, side, 1)
            cond_part(f, both, me)
        else:
            snd_buf[f] = dot(mel[...], both, ((1,), (1,))).astype(BF16)
            for step in range(1, n_dp):
                peer = lax.rem(me + step, n_dp)
                cond_send_block(f, peer, step - 1, whole, peer, step - 1)
        if f > 0:
            grad_mixed = chan_finish(chan_buf.at[NFLOW + f - 1], copies)
            inner = jnp.concatenate([grad_state[:H], grad_second * gain], axis=0) + grad_mixed
            grad_state = jnp.where(valid, dot_tn(mixes[f], inner), 0.0)

    fin_copies = [None] * NFLOW

    def weight_sums(f):
        for copy in sum_copies[f]:
            copy.wait_recv()
        total = sum_buf[f, 0].astype(F32)
        for block in range(1, n_dp):
            total = total + sum_buf[f, block].astype(F32)
        start_part = jnp.zeros((H, res_size), F32)
        n_rows = cat_rows(total)
        ends = jnp.concatenate([total[12:16, :width], total[12:16, width:]], axis=0)
        for tap in range(3):
            block = columns(
                lambda c: w_in[f, :, :, c].reshape(2 * width, c.size if isinstance(c, pl.Slice) else res),
                tap * res,
                me * res_size,
                res_size,
                res,
            )
            r = fold_rows(dot(n_rows, block, ((1,), (0,))))
            start_part = start_part + r[tap * H : tap * H + H]
        block = columns(lambda c: w_skip[f, :, c], 0, me * res_size, res_size, res)
        rows = cat_rows(ends)
        end_part = fold_rows(dot(rows, block, ((1,), (0,))))
        final = jnp.concatenate([start_part, jnp.zeros((8 - H, res_size), F32), end_part], axis=0)
        fin_copies[f] = chan_start(fin_buf.at[f], 2 * NFLOW - 1 + f, final)
        cols = columns_f32(lambda c: basis[f, :, c], me * in_size, in_size, 3 * res)
        o_in[f] = dot_tn(total, cols).reshape(2, width, in_size)
        end_cols = columns_f32(lambda c: w_end_ref[f, :, c], me * res_size, res_size, res)
        o_skip[f] = dot_tn(ends, end_cols)

    def cond_sums(f):
        if n_dp == 4:
            pieces = [(lows[f], {1: 1, 3: 2, 4: 3}), (tops[f], {1: 1, 2: 2})]
        else:
            pieces = [(whole, {at: at for at in range(n_dp - 1)})]
        waited = set()
        for part, slots_of in pieces:
            total = snd_buf[f, block_rows(me, part), :].astype(F32)
            for at, slot in slots_of.items():
                if at not in waited:
                    cond_copies[f][at].wait_recv()
                    waited.add(at)
                total = total + rcv_buf[f, slot, pl.ds(*part)].astype(F32)
            start = part[0]
            rows = min(part[1], o_cond.shape[2] - start)
            o_cond[f, 0, start : start + rows] = total[:rows, :width]
            o_cond[f, 1, start : start + rows] = total[:rows, width:]

    cond_relay(1)
    weight_sums(1)
    cond_relay(0)
    weight_sums(0)
    cond_sums(1)
    for f in reversed(range(NFLOW)):
        final = chan_finish(fin_buf.at[f], fin_copies[f])
        o_start[f] = final[:H]
        o_end[f] = final[8:16]
    cond_sums(0)
    for copy in pending:
        copy.wait_send()


def finish(i_start, i_in, i_cond, i_skip, i_end, o_start, o_in, o_cond, o_skip, o_end, sem):
    copies = [
        pltpu.make_async_copy(src, dst, sem.at[at])
        for at, (src, dst) in enumerate(
            [(i_in, o_in), (i_cond, o_cond), (i_skip, o_skip), (i_end, o_end), (i_start, o_start)]
        )
    ]
    for copy in copies:
        copy.start()
    for copy in copies:
        copy.wait()


def on_device(
    audio,
    mel,
    crop_len,
    pack_offset,
    low_mix,
    up_mix,
    log_scale,
    w_start,
    w_in,
    w_cond,
    w_skip,
    w_end,
):
    n_dp = lax.axis_size("dp")
    n_chan = lax.axis_size("chan")
    groups, _, slots = audio.shape
    channels = mel.shape[0]
    _, _, width, taps = w_in.shape
    res = w_end.shape[2]
    audio = audio.reshape(groups, slots)
    mel = mel.reshape(channels, slots)
    rows = channels // n_dp
    padded = -(-rows // 16) * 16
    if padded != rows:
        mel = jnp.pad(mel.reshape(n_dp, rows, slots), ((0, 0), (0, padded - rows), (0, 0)))
        mel = mel.reshape(n_dp * padded, slots)
        w_cond = jnp.pad(
            w_cond.reshape(NFLOW, 2, width, n_dp, rows),
            ((0, 0), (0, 0), (0, 0), (0, 0), (0, padded - rows)),
        ).reshape(NFLOW, 2, width, n_dp * padded)
    vmem = pl.BlockSpec(memory_space=pltpu.VMEM)
    hbm = pl.BlockSpec(memory_space=pltpu.HBM)
    res_size = res // n_dp
    out_shape = (
        jax.ShapeDtypeStruct((NFLOW, H, res_size), F32),
        jax.ShapeDtypeStruct((NFLOW, 2, width, taps // n_dp), F32),
        jax.ShapeDtypeStruct((NFLOW, 2, rows, width), F32),
        jax.ShapeDtypeStruct((NFLOW, width, res_size), F32),
        jax.ShapeDtypeStruct((NFLOW, 2 * H, res_size), F32),
    )
    results = pl.pallas_call(
        functools.partial(kernel, n_dp, n_chan),
        out_shape=out_shape,
        in_specs=[hbm] * 11,
        out_specs=[vmem] * 5,
        scratch_shapes=[
            pltpu.SMEM(crop_len.shape, jnp.int32),
            pltpu.VMEM(audio.shape, BF16),
            pltpu.VMEM(low_mix.shape, F32),
            pltpu.VMEM(up_mix.shape, F32),
            pltpu.VMEM(log_scale.shape, F32),
            pltpu.VMEM(w_start.shape, F32),
            pltpu.VMEM(w_end.shape, F32),
            pltpu.VMEM(mel.shape, BF16),
            pltpu.VMEM(w_in.shape, BF16),
            pltpu.VMEM(w_cond.shape, BF16),
            pltpu.VMEM(w_skip.shape, BF16),
            pltpu.VMEM((NFLOW, 8, res), F32),
            pltpu.VMEM((NFLOW, 16, 3 * res), F32),
            pltpu.VMEM((NFLOW, 2 * width, slots), F32),
            pltpu.VMEM((2 * NFLOW - 1, n_chan, 8, slots), F32),
            pltpu.VMEM((NFLOW, n_chan, 16, res_size), F32),
            pltpu.VMEM((NFLOW, n_dp, 16, 2 * width), BF16),
            pltpu.VMEM((NFLOW, n_dp * padded, 2 * width), BF16),
            pltpu.VMEM((NFLOW, max(n_dp - 1, 4), padded, 2 * width), BF16),
            pltpu.VMEM((NFLOW, padded, 2 * width), BF16),
            pltpu.SemaphoreType.DMA((13,)),
            pltpu.SemaphoreType.DMA((3 * NFLOW - 1, n_chan)),
            pltpu.SemaphoreType.DMA((3 * NFLOW - 1, n_chan)),
            pltpu.SemaphoreType.DMA((NFLOW, n_dp)),
            pltpu.SemaphoreType.DMA((NFLOW, n_dp)),
            pltpu.SemaphoreType.DMA((NFLOW, max(n_dp, 5))),
            pltpu.SemaphoreType.DMA((NFLOW, max(n_dp, 5))),
            pltpu.SemaphoreType.REGULAR((2,)),
        ],
        compiler_params=pltpu.CompilerParams(
            collective_id=0, has_side_effects=True, vmem_limit_bytes=24 * 1024 * 1024
        ),
        name="flow_steps",
    )(*[
        pltpu.with_memory_space_constraint(a, pltpu.HBM)
        for a in (
            crop_len, audio, low_mix, up_mix, log_scale, w_start, w_end, mel, w_in, w_cond, w_skip
        )
    ])
    g_start, g_in, g_cond, g_skip, g_end = pl.pallas_call(
        finish,
        out_shape=out_shape,
        in_specs=[vmem] * 5,
        out_specs=[hbm] * 5,
        scratch_shapes=[pltpu.SemaphoreType.DMA((5,))],
        compiler_params=pltpu.CompilerParams(vmem_limit_bytes=16 * 1024 * 1024),
        name="finish",
    )(*results)
    return g_start, g_in, jnp.swapaxes(g_cond, 2, 3), g_skip, g_end


def solution(mesh):
    in_specs = (
        P(None, ("group", "dp"), None),
        P(None, ("group", "dp"), None),
        P("group", None),
        P("group", None),
        P(),
        P(),
        P(),
        P(),
        P(None, None, "chan", None),
        P(None, None, "chan", None),
        P(None, "chan", None),
        P(),
    )
    out_specs = (
        P("group", None, "dp"),
        P("group", None, "chan", "dp"),
        P("group", None, "chan", "dp"),
        P("group", "chan", "dp"),
        P("group", None, "dp"),
    )
    return jax.shard_map(
        on_device, mesh=mesh, in_specs=in_specs, out_specs=out_specs, check_vma=False
    )
```

```python
import functools
import math

import jax
import jax.numpy as jnp
from jax import lax
from jax.experimental import pallas as pl
from jax.experimental.pallas import tpu as pltpu
from jax.sharding import PartitionSpec as P

H = 4
NFLOW = 2
PACK = 256
MESH = pl.DeviceIdType.MESH
F32 = jnp.float32
BF16 = jnp.bfloat16


def dot(a, b, dims):
    return lax.dot_general(a, b, (dims, ((), ())), preferred_element_type=F32)


def halves(a):
    high = a.astype(BF16).astype(F32)
    return high, a - high


def cat_left(a):
    high, low = halves(a)
    return jnp.concatenate([high, high, low], axis=0).astype(BF16)


def cat_right(b):
    high, low = halves(b)
    return jnp.concatenate([high, low, high], axis=0).astype(BF16)


def dot_tn(a, b):
    return dot(cat_left(a), cat_right(b), ((0,), (0,)))


def cat_rows(a):
    high, low = halves(a)
    return jnp.concatenate([high, low], axis=0).astype(BF16)


def fold_rows(r):
    half = r.shape[0] // 2
    return r[:half] + r[half:]


def fold_lanes(a):
    half = a.shape[1] // 2
    return jnp.concatenate([a[:, :half], a[:, half:]], axis=0)


def spread_lanes(a):
    half = a.shape[0] // 2
    return jnp.concatenate([a[:half], a[half:]], axis=1)


def columns(read, base, start, size, full):
    if size % 128 == 0:
        return read(pl.ds(pl.multiple_of(base + start, 128), size))
    row = lax.broadcasted_iota(jnp.int32, (full, size), 0)
    col = lax.broadcasted_iota(jnp.int32, (full, size), 1)
    pick = jnp.where(row == col + start, 1.0, 0.0).astype(BF16)
    return dot(read(slice(base, base + full)), pick, ((1,), (0,))).astype(BF16)


def columns_f32(read, start, size, full):
    if size % 128 == 0:
        return read(pl.ds(pl.multiple_of(start, 128), size))
    row = lax.broadcasted_iota(jnp.int32, (full, size), 0)
    col = lax.broadcasted_iota(jnp.int32, (full, size), 1)
    pick = jnp.where(row == col + start, 1.0, 0.0).astype(BF16)
    return fold_rows(dot(cat_rows(read(slice(None))), pick, ((1,), (0,))))


def kernel(
    n_dp,
    n_chan,
    len_hbm,
    audio_hbm,
    low_hbm,
    up_hbm,
    scale_hbm,
    w_start_hbm,
    w_end_hbm,
    mel_hbm,
    w_in_hbm,
    w_cond_hbm,
    w_skip_hbm,
    o_start,
    o_in,
    o_cond,
    o_skip,
    o_end,
    len_ref,
    audio_ref,
    low_ref,
    up_ref,
    scale_ref,
    w_start_ref,
    w_end_ref,
    mel,
    w_in,
    w_cond,
    w_skip,
    w_first,
    basis,
    cond,
    chan_buf,
    back_buf,
    fin_buf,
    sum_buf,
    snd_buf,
    rcv_buf,
    fwd_buf,
    load_sem,
    chan_send,
    chan_recv,
    sum_send,
    sum_recv,
    cond_send,
    cond_recv,
    go,
):
    slots = audio_ref.shape[1]
    cap = slots // n_dp
    width = w_in_hbm.shape[2]
    res = w_end_ref.shape[2]
    mel_rows = mel_hbm.shape[0] // n_dp
    res_size = o_skip.shape[2]
    in_size = o_in.shape[3]
    obj_scale = 8.0 / math.sqrt(n_dp * PACK)
    me = lax.axis_index("dp")
    chan = lax.axis_index("chan")

    barrier = pltpu.get_barrier_semaphore()
    split = n_chan == 4
    core = lax.rem(chan, 2)
    even, odd = chan - core, chan - core + 1

    def signal(semaphore, **device):
        pl.semaphore_signal(semaphore, inc=1, device_id=device, device_id_type=MESH)

    if split:
        signal(barrier, chan=lax.rem(even + 2, n_chan))

        @pl.when(core == 1)
        def _():
            signal(barrier, chan=even)
    else:
        for step in range(1, n_chan):
            signal(barrier, chan=lax.rem(chan + step, n_chan))
        for step in range(1, n_dp):
            signal(barrier, dp=lax.rem(me + step, n_dp))

    def chan_ready():
        if not split:
            pl.semaphore_wait(barrier, n_chan + n_dp - 2)
            return

        @pl.when(core == 0)
        def _():
            pl.semaphore_wait(barrier, n_chan - 1)
            signal(go.at[0], chan=odd)

        @pl.when(core == 1)
        def _():
            pl.semaphore_wait(go.at[0], 1)

    def dp_ready():
        if not split:
            return

        @pl.when(core == 1)
        def _():
            pl.semaphore_wait(barrier, 2 * (n_dp - 1))
            signal(go.at[1], chan=even)

        @pl.when(core == 0)
        def _():
            pl.semaphore_wait(go.at[1], 1)

    pairs = {
        "start": (w_start_hbm, w_start_ref),
        "in0": (w_in_hbm.at[0], w_in.at[0]),
        "len": (len_hbm, len_ref),
        "audio": (audio_hbm, audio_ref),
        "low": (low_hbm, low_ref),
        "up": (up_hbm, up_ref),
        "scale": (scale_hbm, scale_ref),
        "end": (w_end_hbm, w_end_ref),
        "skip": (w_skip_hbm, w_skip),
        "mel": (mel_hbm, mel),
        "cond0": (w_cond_hbm.at[0], w_cond.at[0]),
        "in1": (w_in_hbm.at[1], w_in.at[1]),
        "cond1": (w_cond_hbm.at[1], w_cond.at[1]),
    }
    loads = {
        key: pltpu.make_async_copy(src, dst, load_sem.at[at])
        for at, (key, (src, dst)) in enumerate(pairs.items())
    }
    for load in loads.values():
        load.start()
    if split:
        for step in range(1, n_dp):
            signal(barrier, dp=lax.rem(me + step, n_dp), chan=odd)

    def chan_start(buf, phase, value):
        buf[chan] = value
        copies = [
            pltpu.make_async_remote_copy(
                src_ref=buf.at[chan],
                dst_ref=buf.at[chan],
                send_sem=chan_send.at[phase, step],
                recv_sem=chan_recv.at[phase, step],
                device_id={"chan": lax.rem(chan + step, n_chan)},
                device_id_type=MESH,
            )
            for step in sorted(range(1, n_chan), key=lambda step: abs(2 * step - n_chan))
        ]
        for copy in copies:
            copy.start()
        pending.extend(copies)
        return copies

    def chan_finish(buf, copies):
        for copy in copies:
            copy.wait_recv()
        total = buf[0].astype(F32)
        for block in range(1, n_chan):
            total = total + buf[block].astype(F32)
        return total

    pending = []
    w_first[...] = jnp.zeros(w_first.shape, F32)
    basis[...] = jnp.zeros(basis.shape, F32)

    for key in ("len", "audio", "low", "up", "scale"):
        loads[key].wait()
    column = lax.broadcasted_iota(jnp.int32, (8, slots), 1)
    owner = column // cap
    within = column - owner * cap
    lens = jnp.zeros((8, slots), jnp.int32)
    for block in range(n_dp):
        lens = jnp.where(owner == block, len_ref[block, me], lens)
    valid = within < lens
    prev_mask = valid & (within >= 1)
    next_mask = within + 1 < lens

    row8 = lax.broadcasted_iota(jnp.int32, (8, 8), 0)
    col8 = lax.broadcasted_iota(jnp.int32, (8, 8), 1)
    mixes = []
    for f in range(NFLOW):
        lower = jnp.where(row8 > col8, low_ref[f], jnp.where(row8 == col8, 1.0, 0.0))
        diag = jnp.broadcast_to(jnp.exp(scale_ref[f : f + 1, :]), (8, 8))
        upper = jnp.where(row8 < col8, up_ref[f], jnp.where(row8 == col8, diag, 0.0))
        mixing = lower[:, 0:1] * upper[0:1, :]
        for k in range(1, 8):
            mixing = mixing + lower[:, k : k + 1] * upper[k : k + 1, :]
        mixes.append(mixing)

    def mix(f, x):
        mixing = mixes[f]
        mixed = mixing[:, 0:1] * x[0:1, :]
        for k in range(1, 8):
            mixed = mixed + mixing[:, k : k + 1] * x[k : k + 1, :]
        return mixed

    w_eff = [None] * NFLOW
    b_skip = [None] * NFLOW

    def precompute(f):
        loads["in%d" % f].wait()
        start16 = cat_rows(w_first[f])
        taps = []
        for tap in range(3):
            block = w_in[f, :, :, tap * res : (tap + 1) * res].reshape(2 * width, res)
            taps.append(fold_rows(dot(start16, block, ((1,), (1,)))))
        w_eff[f] = jnp.concatenate(taps, axis=0)
        if f == 0:
            loads["end"].wait()
            loads["skip"].wait()
        b_skip[f] = fold_rows(dot(cat_rows(w_end_ref[f]), w_skip[f], ((1,), (1,))))
        if f == 0:
            loads["mel"].wait()
        loads["cond%d" % f].wait()
        every = w_cond[f].reshape(2 * width, w_cond.shape[3])
        cond[f] = dot(every, mel[...], ((1,), (0,)))

    x_state = jnp.where(valid, audio_ref[...].astype(F32), 0.0)
    loads["start"].wait()
    for f in range(NFLOW):
        w_first[f, :H] = w_start_ref[f]
    precompute(0)
    saved = []
    for f in range(NFLOW):
        mixed = mix(f, x_state)
        stacked = jnp.concatenate(
            [
                jnp.where(prev_mask, pltpu.roll(mixed, 1, 1), 0.0),
                mixed,
                jnp.where(next_mask, pltpu.roll(mixed, slots - 1, 1), 0.0),
            ],
            axis=0,
        )
        pre = dot_tn(w_eff[f], stacked) + cond[f]
        tanh_val = jnp.tanh(pre[:width])
        sigm_val = 0.5 * jnp.tanh(0.5 * pre[width:]) + 0.5
        gated = (tanh_val * sigm_val).astype(BF16)
        part = fold_rows(dot(cat_rows(b_skip[f]), gated, ((1,), (0,))))
        if f == 0:
            chan_ready()
        copies = chan_start(chan_buf.at[f], f, fold_lanes(part).astype(BF16))
        if f == 0:
            precompute(1)
            for g in range(NFLOW):
                for tap in range(3):
                    basis[g, tap * H : tap * H + H, tap * res : (tap + 1) * res] = w_start_ref[g]
        slope_tanh = sigm_val * (1.0 - tanh_val * tanh_val)
        slope_sigm = tanh_val * sigm_val * (1.0 - sigm_val)
        coupling = spread_lanes(chan_finish(chan_buf.at[f], copies))
        gain = jnp.exp(coupling[:H])
        second = mixed[H:]
        saved.append((mixed, stacked, slope_tanh, slope_sigm, gated, gain))
        x_state = jnp.where(
            valid, jnp.concatenate([mixed[:H], gain * second + coupling[H:]], axis=0), 0.0
        )

    side = me + 1 - 2 * lax.rem(me, 2)
    far = lax.rem(me + 2, n_dp)
    diag = lax.rem(side + 2, n_dp)
    tops = [(0, mel_rows * 64 // 160 // 16 * 16), (0, mel_rows * 80 // 160 // 16 * 16)]
    lows = [(size, mel_rows - size) for _, size in tops]
    whole = (0, mel_rows)

    def block_rows(block, part=whole):
        start, size = part
        return pl.ds(pl.multiple_of(block * mel_rows + start, 16), size)

    def cond_start(f, source, slot, part, peer, at):
        copy = pltpu.make_async_remote_copy(
            src_ref=source,
            dst_ref=rcv_buf.at[f, slot, pl.ds(*part)],
            send_sem=cond_send.at[f, at],
            recv_sem=cond_recv.at[f, at],
            device_id={"dp": peer},
            device_id_type=MESH,
        )
        copy.start()
        pending.append(copy)
        cond_copies[f][at] = copy

    def cond_send_block(f, block, slot, part, peer, at):
        cond_start(f, snd_buf.at[f, block_rows(block, part)], slot, part, peer, at)

    def cond_part(f, both, block):
        rows = block_rows(block)
        snd_buf[f, rows, :] = dot(mel[rows, :], both, ((1,), (1,))).astype(BF16)

    def sum_copy(f, source, slot, peer, at):
        copy = pltpu.make_async_remote_copy(
            src_ref=source,
            dst_ref=sum_buf.at[f, slot],
            send_sem=sum_send.at[f, at],
            recv_sem=sum_recv.at[f, at],
            device_id={"dp": peer},
            device_id_type=MESH,
        )
        copy.start()
        return copy

    def sum_relay(f):
        if n_dp != 4:
            return
        sum_copies[f][0].wait_recv()
        pair = sum_buf[f, me].astype(F32) + sum_buf[f, side].astype(F32)
        sum_buf[f, far] = pair.astype(BF16)
        copy = sum_copy(f, sum_buf.at[f, far], diag, far, 1)
        sum_copies[f].append(copy)
        pending.append(copy)

    def cond_relay(f):
        if n_dp != 4:
            return
        top = tops[f]
        cond_copies[f][0].wait_recv()
        total = snd_buf[f, block_rows(far, top), :].astype(F32) + rcv_buf[f, 0, pl.ds(*top)].astype(F32)
        fwd_buf[f, pl.ds(*top)] = total.astype(BF16)
        cond_start(f, fwd_buf.at[f, pl.ds(*top)], 2, top, far, 2)

    grad_state = obj_scale * x_state
    sum_copies = [None] * NFLOW
    cond_copies = [{} for _ in range(NFLOW)]
    for f in reversed(range(NFLOW)):
        mixed, stacked, slope_tanh, slope_sigm, gated, gain = saved[f]
        grad_second = grad_state[H:]
        grad_log = grad_second * gain * mixed[H:] - obj_scale
        grad_coupling = jnp.where(
            valid, jnp.concatenate([grad_log, grad_second], axis=0), 0.0
        )
        grad_gated = dot_tn(b_skip[f], grad_coupling)
        grad_tanh = (grad_gated * slope_tanh).astype(BF16)
        grad_sigm = (grad_gated * slope_sigm).astype(BF16)
        both = jnp.concatenate([grad_tanh, grad_sigm], axis=0)
        if f > 0:
            back = fold_rows(dot(cat_rows(w_eff[f]), both, ((1,), (0,))))
            part = (
                back[8:16]
                + pltpu.roll(jnp.where(prev_mask, back[0:8], 0.0), slots - 1, 1)
                + pltpu.roll(jnp.where(next_mask, back[16:24], 0.0), 1, 1)
            )
            copies = chan_start(back_buf, NFLOW + f - 1, fold_lanes(part[:H]))
        left = cat_rows(jnp.concatenate([stacked, grad_coupling], axis=0))
        values = jnp.concatenate([both, gated], axis=0)
        r = fold_rows(dot(left, values, ((1,), (1,))))
        n_part = jnp.concatenate([r[0:4], r[8:12], r[16:20]], axis=0)[:, : 2 * width]
        m_part = jnp.concatenate([r[24:28, 2 * width :], r[28:32, 2 * width :]], axis=1)
        sum_buf[f, me] = jnp.concatenate([n_part, m_part], axis=0).astype(BF16)
        if f == NFLOW - 1:
            dp_ready()
        relay = False
        sum_copies[f] = [
            sum_copy(f, sum_buf.at[f, me], me, peer, at)
            for at, peer in enumerate(
                [side] if relay else [lax.rem(me + step, n_dp) for step in range(1, n_dp)]
            )
        ]
        pending += sum_copies[f]
        if n_dp == 4:
            cond_part(f, both, diag)
            cond_send_block(f, diag, 0, tops[f], side, 0)
            cond_send_block(f, diag, 3, lows[f], diag, 4)
        if n_dp == 4:
            cond_part(f, both, far)
            cond_send_block(f, far, 2, lows[f], far, 3)
            cond_part(f, both, side)
            cond_send_block(f, side, 1, whole, side, 1)
            cond_part(f, both, me)
        else:
            snd_buf[f] = dot(mel[...], both, ((1,), (1,))).astype(BF16)
            for step in range(1, n_dp):
                peer = lax.rem(me + step, n_dp)
                cond_send_block(f, peer, step - 1, whole, peer, step - 1)
        if f > 0:
            grad_first = grad_state[:H] + spread_lanes(chan_finish(back_buf, copies))
            inner = jnp.concatenate([grad_first, grad_second * gain], axis=0)
            grad_state = jnp.where(valid, dot_tn(mixes[f], inner), 0.0)

    fin_copies = [None] * NFLOW

    def weight_sums(f):
        for copy in sum_copies[f]:
            copy.wait_recv()
        total = sum_buf[f, 0].astype(F32)
        for block in range(1, n_dp):
            total = total + sum_buf[f, block].astype(F32)
        start_part = jnp.zeros((H, res_size), F32)
        n_rows = cat_rows(total)
        ends = jnp.concatenate([total[12:16, :width], total[12:16, width:]], axis=0)
        for tap in range(3):
            block = columns(
                lambda c: w_in[f, :, :, c].reshape(2 * width, c.size if isinstance(c, pl.Slice) else res),
                tap * res,
                me * res_size,
                res_size,
                res,
            )
            r = fold_rows(dot(n_rows, block, ((1,), (0,))))
            start_part = start_part + r[tap * H : tap * H + H]
        block = columns(lambda c: w_skip[f, :, c], 0, me * res_size, res_size, res)
        rows = cat_rows(ends)
        end_part = fold_rows(dot(rows, block, ((1,), (0,))))
        final = jnp.concatenate([start_part, jnp.zeros((8 - H, res_size), F32), end_part], axis=0)
        fin_copies[f] = chan_start(fin_buf.at[f], 2 * NFLOW - 1 + f, final)
        cols = columns_f32(lambda c: basis[f, :, c], me * in_size, in_size, 3 * res)
        o_in[f] = dot_tn(total, cols).reshape(2, width, in_size)
        end_cols = columns_f32(lambda c: w_end_ref[f, :, c], me * res_size, res_size, res)
        o_skip[f] = dot_tn(ends, end_cols)

    def cond_sums(f):
        if n_dp == 4:
            pieces = [(lows[f], {1: 1, 3: 2, 4: 3}), (tops[f], {1: 1, 2: 2})]
        else:
            pieces = [(whole, {at: at for at in range(n_dp - 1)})]
        waited = set()
        for part, slots_of in pieces:
            total = snd_buf[f, block_rows(me, part), :].astype(F32)
            for at, slot in slots_of.items():
                if at not in waited:
                    cond_copies[f][at].wait_recv()
                    waited.add(at)
                total = total + rcv_buf[f, slot, pl.ds(*part)].astype(F32)
            start = part[0]
            rows = min(part[1], o_cond.shape[2] - start)
            o_cond[f, 0, start : start + rows] = total[:rows, :width]
            o_cond[f, 1, start : start + rows] = total[:rows, width:]

    cond_relay(1)
    weight_sums(1)
    cond_relay(0)
    weight_sums(0)
    cond_sums(1)
    for f in reversed(range(NFLOW)):
        final = chan_finish(fin_buf.at[f], fin_copies[f])
        o_start[f] = final[:H]
        o_end[f] = final[8:16]
    cond_sums(0)
    for copy in pending:
        copy.wait_send()


def finish(i_start, i_in, i_cond, i_skip, i_end, o_start, o_in, o_cond, o_skip, o_end, sem):
    copies = [
        pltpu.make_async_copy(src, dst, sem.at[at])
        for at, (src, dst) in enumerate(
            [(i_in, o_in), (i_cond, o_cond), (i_skip, o_skip), (i_end, o_end), (i_start, o_start)]
        )
    ]
    for copy in copies:
        copy.start()
    for copy in copies:
        copy.wait()


def on_device(
    audio,
    mel,
    crop_len,
    pack_offset,
    low_mix,
    up_mix,
    log_scale,
    w_start,
    w_in,
    w_cond,
    w_skip,
    w_end,
):
    n_dp = lax.axis_size("dp")
    n_chan = lax.axis_size("chan")
    groups, _, slots = audio.shape
    channels = mel.shape[0]
    _, _, width, taps = w_in.shape
    res = w_end.shape[2]
    audio = audio.reshape(groups, slots)
    mel = mel.reshape(channels, slots)
    rows = channels // n_dp
    padded = -(-rows // 16) * 16
    if padded != rows:
        mel = jnp.pad(mel.reshape(n_dp, rows, slots), ((0, 0), (0, padded - rows), (0, 0)))
        mel = mel.reshape(n_dp * padded, slots)
        w_cond = jnp.pad(
            w_cond.reshape(NFLOW, 2, width, n_dp, rows),
            ((0, 0), (0, 0), (0, 0), (0, 0), (0, padded - rows)),
        ).reshape(NFLOW, 2, width, n_dp * padded)
    vmem = pl.BlockSpec(memory_space=pltpu.VMEM)
    hbm = pl.BlockSpec(memory_space=pltpu.HBM)
    res_size = res // n_dp
    out_shape = (
        jax.ShapeDtypeStruct((NFLOW, H, res_size), F32),
        jax.ShapeDtypeStruct((NFLOW, 2, width, taps // n_dp), F32),
        jax.ShapeDtypeStruct((NFLOW, 2, rows, width), F32),
        jax.ShapeDtypeStruct((NFLOW, width, res_size), F32),
        jax.ShapeDtypeStruct((NFLOW, 2 * H, res_size), F32),
    )
    results = pl.pallas_call(
        functools.partial(kernel, n_dp, n_chan),
        out_shape=out_shape,
        in_specs=[hbm] * 11,
        out_specs=[vmem] * 5,
        scratch_shapes=[
            pltpu.SMEM(crop_len.shape, jnp.int32),
            pltpu.VMEM(audio.shape, BF16),
            pltpu.VMEM(low_mix.shape, F32),
            pltpu.VMEM(up_mix.shape, F32),
            pltpu.VMEM(log_scale.shape, F32),
            pltpu.VMEM(w_start.shape, F32),
            pltpu.VMEM(w_end.shape, F32),
            pltpu.VMEM(mel.shape, BF16),
            pltpu.VMEM(w_in.shape, BF16),
            pltpu.VMEM(w_cond.shape, BF16),
            pltpu.VMEM(w_skip.shape, BF16),
            pltpu.VMEM((NFLOW, 8, res), F32),
            pltpu.VMEM((NFLOW, 16, 3 * res), F32),
            pltpu.VMEM((NFLOW, 2 * width, slots), F32),
            pltpu.VMEM((NFLOW, n_chan, 16, slots // 2), BF16),
            pltpu.VMEM((n_chan, 8, slots // 2), F32),
            pltpu.VMEM((NFLOW, n_chan, 16, res_size), F32),
            pltpu.VMEM((NFLOW, n_dp, 16, 2 * width), BF16),
            pltpu.VMEM((NFLOW, n_dp * padded, 2 * width), BF16),
            pltpu.VMEM((NFLOW, max(n_dp - 1, 4), padded, 2 * width), BF16),
            pltpu.VMEM((NFLOW, padded, 2 * width), BF16),
            pltpu.SemaphoreType.DMA((13,)),
            pltpu.SemaphoreType.DMA((3 * NFLOW - 1, n_chan)),
            pltpu.SemaphoreType.DMA((3 * NFLOW - 1, n_chan)),
            pltpu.SemaphoreType.DMA((NFLOW, n_dp)),
            pltpu.SemaphoreType.DMA((NFLOW, n_dp)),
            pltpu.SemaphoreType.DMA((NFLOW, max(n_dp, 5))),
            pltpu.SemaphoreType.DMA((NFLOW, max(n_dp, 5))),
            pltpu.SemaphoreType.REGULAR((2,)),
        ],
        compiler_params=pltpu.CompilerParams(
            collective_id=0, has_side_effects=True, vmem_limit_bytes=24 * 1024 * 1024
        ),
        name="flow_steps",
    )(*[
        pltpu.with_memory_space_constraint(a, pltpu.HBM)
        for a in (
            crop_len, audio, low_mix, up_mix, log_scale, w_start, w_end, mel, w_in, w_cond, w_skip
        )
    ])
    g_start, g_in, g_cond, g_skip, g_end = pl.pallas_call(
        finish,
        out_shape=out_shape,
        in_specs=[vmem] * 5,
        out_specs=[hbm] * 5,
        scratch_shapes=[pltpu.SemaphoreType.DMA((5,))],
        compiler_params=pltpu.CompilerParams(vmem_limit_bytes=16 * 1024 * 1024),
        name="finish",
    )(*results)
    return g_start, g_in, jnp.swapaxes(g_cond, 2, 3), g_skip, g_end


def solution(mesh):
    in_specs = (
        P(None, ("group", "dp"), None),
        P(None, ("group", "dp"), None),
        P("group", None),
        P("group", None),
        P(),
        P(),
        P(),
        P(),
        P(None, None, "chan", None),
        P(None, None, "chan", None),
        P(None, "chan", None),
        P(),
    )
    out_specs = (
        P("group", None, "dp"),
        P("group", None, "chan", "dp"),
        P("group", None, "chan", "dp"),
        P("group", "chan", "dp"),
        P("group", None, "dp"),
    )
    return jax.shard_map(
        on_device, mesh=mesh, in_specs=in_specs, out_specs=out_specs, check_vma=False
    )
```

```python
import functools
import math

import jax
import jax.numpy as jnp
from jax import lax
from jax.experimental import pallas as pl
from jax.experimental.pallas import tpu as pltpu
from jax.sharding import PartitionSpec as P

H = 4
NFLOW = 2
PACK = 256
MESH = pl.DeviceIdType.MESH
F32 = jnp.float32
BF16 = jnp.bfloat16


def dot(a, b, dims):
    return lax.dot_general(a, b, (dims, ((), ())), preferred_element_type=F32)


def halves(a):
    high = a.astype(BF16).astype(F32)
    return high, a - high


def cat_left(a):
    high, low = halves(a)
    return jnp.concatenate([high, high, low], axis=0).astype(BF16)


def cat_right(b):
    high, low = halves(b)
    return jnp.concatenate([high, low, high], axis=0).astype(BF16)


def dot_tn(a, b):
    return dot(cat_left(a), cat_right(b), ((0,), (0,)))


def cat_rows(a):
    high, low = halves(a)
    return jnp.concatenate([high, low], axis=0).astype(BF16)


def fold_rows(r):
    half = r.shape[0] // 2
    return r[:half] + r[half:]


def fold_lanes(a):
    half = a.shape[1] // 2
    return jnp.concatenate([a[:, :half], a[:, half:]], axis=0)


def spread_lanes(a):
    half = a.shape[0] // 2
    return jnp.concatenate([a[:half], a[half:]], axis=1)


def columns(read, base, start, size, full):
    if size % 128 == 0:
        return read(pl.ds(pl.multiple_of(base + start, 128), size))
    row = lax.broadcasted_iota(jnp.int32, (full, size), 0)
    col = lax.broadcasted_iota(jnp.int32, (full, size), 1)
    pick = jnp.where(row == col + start, 1.0, 0.0).astype(BF16)
    return dot(read(slice(base, base + full)), pick, ((1,), (0,))).astype(BF16)


def columns_f32(read, start, size, full):
    if size % 128 == 0:
        return read(pl.ds(pl.multiple_of(start, 128), size))
    row = lax.broadcasted_iota(jnp.int32, (full, size), 0)
    col = lax.broadcasted_iota(jnp.int32, (full, size), 1)
    pick = jnp.where(row == col + start, 1.0, 0.0).astype(BF16)
    return fold_rows(dot(cat_rows(read(slice(None))), pick, ((1,), (0,))))


def kernel(
    n_dp,
    n_chan,
    len_hbm,
    audio_hbm,
    low_hbm,
    up_hbm,
    scale_hbm,
    w_start_hbm,
    w_end_hbm,
    mel_hbm,
    w_in_hbm,
    w_cond_hbm,
    w_skip_hbm,
    o_start,
    o_in,
    o_cond,
    o_skip,
    o_end,
    len_ref,
    audio_ref,
    low_ref,
    up_ref,
    scale_ref,
    w_start_ref,
    w_end_ref,
    mel,
    w_in,
    w_cond,
    w_skip,
    w_first,
    basis,
    cond,
    chan_buf,
    back_buf,
    fin_buf,
    sum_buf,
    snd_buf,
    rcv_buf,
    fwd_buf,
    load_sem,
    chan_send,
    chan_recv,
    sum_send,
    sum_recv,
    cond_send,
    cond_recv,
    go,
):
    slots = audio_ref.shape[1]
    cap = slots // n_dp
    width = w_in_hbm.shape[2]
    res = w_end_ref.shape[2]
    mel_rows = mel_hbm.shape[0] // n_dp
    res_size = o_skip.shape[2]
    in_size = o_in.shape[3]
    obj_scale = 8.0 / math.sqrt(n_dp * PACK)
    me = lax.axis_index("dp")
    chan = lax.axis_index("chan")

    barrier = pltpu.get_barrier_semaphore()
    split = n_chan == 4
    core = lax.rem(chan, 2)
    even, odd = chan - core, chan - core + 1

    def signal(semaphore, **device):
        pl.semaphore_signal(semaphore, inc=1, device_id=device, device_id_type=MESH)

    if split:
        signal(barrier, chan=lax.rem(even + 2, n_chan))

        @pl.when(core == 1)
        def _():
            signal(barrier, chan=even)
    else:
        for step in range(1, n_chan):
            signal(barrier, chan=lax.rem(chan + step, n_chan))
        for step in range(1, n_dp):
            signal(barrier, dp=lax.rem(me + step, n_dp))

    def chan_ready():
        if not split:
            pl.semaphore_wait(barrier, n_chan + n_dp - 2)
            return

        @pl.when(core == 0)
        def _():
            pl.semaphore_wait(barrier, n_chan - 1)
            signal(go.at[0], chan=odd)

        @pl.when(core == 1)
        def _():
            pl.semaphore_wait(go.at[0], 1)

    def dp_ready():
        if not split:
            return

        @pl.when(core == 1)
        def _():
            pl.semaphore_wait(barrier, 2 * (n_dp - 1))
            signal(go.at[1], chan=even)

        @pl.when(core == 0)
        def _():
            pl.semaphore_wait(go.at[1], 1)

    pairs = {
        "start": (w_start_hbm, w_start_ref),
        "in0": (w_in_hbm.at[0], w_in.at[0]),
        "len": (len_hbm, len_ref),
        "audio": (audio_hbm, audio_ref),
        "low": (low_hbm, low_ref),
        "up": (up_hbm, up_ref),
        "scale": (scale_hbm, scale_ref),
        "end": (w_end_hbm, w_end_ref),
        "skip": (w_skip_hbm, w_skip),
        "mel": (mel_hbm, mel),
        "cond0": (w_cond_hbm.at[0], w_cond.at[0]),
        "in1": (w_in_hbm.at[1], w_in.at[1]),
        "cond1": (w_cond_hbm.at[1], w_cond.at[1]),
    }
    loads = {
        key: pltpu.make_async_copy(src, dst, load_sem.at[at])
        for at, (key, (src, dst)) in enumerate(pairs.items())
    }
    for load in loads.values():
        load.start()
    if split:
        for step in range(1, n_dp):
            signal(barrier, dp=lax.rem(me + step, n_dp), chan=odd)

    def chan_start(buf, phase, value):
        buf[chan] = value
        copies = [
            pltpu.make_async_remote_copy(
                src_ref=buf.at[chan],
                dst_ref=buf.at[chan],
                send_sem=chan_send.at[phase, step],
                recv_sem=chan_recv.at[phase, step],
                device_id={"chan": lax.rem(chan + step, n_chan)},
                device_id_type=MESH,
            )
            for step in sorted(range(1, n_chan), key=lambda step: abs(2 * step - n_chan))
        ]
        for copy in copies:
            copy.start()
        pending.extend(copies)
        return copies

    def chan_finish(buf, copies):
        for copy in copies:
            copy.wait_recv()
        total = buf[0].astype(F32)
        for block in range(1, n_chan):
            total = total + buf[block].astype(F32)
        return total

    pending = []
    w_first[...] = jnp.zeros(w_first.shape, F32)
    basis[...] = jnp.zeros(basis.shape, F32)

    for key in ("len", "audio", "low", "up", "scale"):
        loads[key].wait()
    column = lax.broadcasted_iota(jnp.int32, (8, slots), 1)
    owner = column // cap
    within = column - owner * cap
    lens = jnp.zeros((8, slots), jnp.int32)
    for block in range(n_dp):
        lens = jnp.where(owner == block, len_ref[block, me], lens)
    valid = within < lens
    prev_mask = valid & (within >= 1)
    next_mask = within + 1 < lens

    row8 = lax.broadcasted_iota(jnp.int32, (8, 8), 0)
    col8 = lax.broadcasted_iota(jnp.int32, (8, 8), 1)
    mixes = []
    for f in range(NFLOW):
        lower = jnp.where(row8 > col8, low_ref[f], jnp.where(row8 == col8, 1.0, 0.0))
        diag = jnp.broadcast_to(jnp.exp(scale_ref[f : f + 1, :]), (8, 8))
        upper = jnp.where(row8 < col8, up_ref[f], jnp.where(row8 == col8, diag, 0.0))
        mixing = lower[:, 0:1] * upper[0:1, :]
        for k in range(1, 8):
            mixing = mixing + lower[:, k : k + 1] * upper[k : k + 1, :]
        mixes.append(mixing)

    def mix(f, x):
        mixing = mixes[f]
        mixed = mixing[:, 0:1] * x[0:1, :]
        for k in range(1, 8):
            mixed = mixed + mixing[:, k : k + 1] * x[k : k + 1, :]
        return mixed

    w_eff = [None] * NFLOW
    b_skip = [None] * NFLOW

    def precompute(f):
        loads["in%d" % f].wait()
        start16 = cat_rows(w_first[f])
        taps = []
        for tap in range(3):
            block = w_in[f, :, :, tap * res : (tap + 1) * res].reshape(2 * width, res)
            taps.append(fold_rows(dot(start16, block, ((1,), (1,)))))
        w_eff[f] = jnp.concatenate(taps, axis=0)
        if f == 0:
            loads["end"].wait()
            loads["skip"].wait()
        b_skip[f] = fold_rows(dot(cat_rows(w_end_ref[f]), w_skip[f], ((1,), (1,))))
        if f == 0:
            loads["mel"].wait()
        loads["cond%d" % f].wait()
        every = w_cond[f].reshape(2 * width, w_cond.shape[3])
        cond[f] = dot(every, mel[...], ((1,), (0,)))

    x_state = jnp.where(valid, audio_ref[...].astype(F32), 0.0)
    loads["start"].wait()
    for f in range(NFLOW):
        w_first[f, :H] = w_start_ref[f]
    precompute(0)
    saved = []
    for f in range(NFLOW):
        mixed = mix(f, x_state)
        stacked = jnp.concatenate(
            [
                jnp.where(prev_mask, pltpu.roll(mixed, 1, 1), 0.0),
                mixed,
                jnp.where(next_mask, pltpu.roll(mixed, slots - 1, 1), 0.0),
            ],
            axis=0,
        )
        pre = dot_tn(w_eff[f], stacked) + cond[f]
        tanh_val = jnp.tanh(pre[:width])
        sigm_val = 0.5 * jnp.tanh(0.5 * pre[width:]) + 0.5
        gated = (tanh_val * sigm_val).astype(BF16)
        part = fold_rows(dot(cat_rows(b_skip[f]), gated, ((1,), (0,))))
        if f == 0:
            chan_ready()
        copies = chan_start(chan_buf.at[f], f, fold_lanes(part).astype(BF16))
        if f == 0:
            precompute(1)
            for g in range(NFLOW):
                for tap in range(3):
                    basis[g, tap * H : tap * H + H, tap * res : (tap + 1) * res] = w_start_ref[g]
        slope_tanh = sigm_val * (1.0 - tanh_val * tanh_val)
        slope_sigm = tanh_val * sigm_val * (1.0 - sigm_val)
        coupling = spread_lanes(chan_finish(chan_buf.at[f], copies))
        gain = jnp.exp(coupling[:H])
        second = mixed[H:]
        saved.append((mixed, stacked, slope_tanh, slope_sigm, gated, gain))
        x_state = jnp.where(
            valid, jnp.concatenate([mixed[:H], gain * second + coupling[H:]], axis=0), 0.0
        )

    side = me + 1 - 2 * lax.rem(me, 2)
    far = lax.rem(me + 2, n_dp)
    diag = lax.rem(side + 2, n_dp)
    tops = [(0, mel_rows * 64 // 160 // 16 * 16), (0, mel_rows * 80 // 160 // 16 * 16)]
    lows = [(size, mel_rows - size) for _, size in tops]
    whole = (0, mel_rows)

    def block_rows(block, part=whole):
        start, size = part
        return pl.ds(pl.multiple_of(block * mel_rows + start, 16), size)

    def cond_start(f, source, slot, part, peer, at):
        copy = pltpu.make_async_remote_copy(
            src_ref=source,
            dst_ref=rcv_buf.at[f, slot, pl.ds(*part)],
            send_sem=cond_send.at[f, at],
            recv_sem=cond_recv.at[f, at],
            device_id={"dp": peer},
            device_id_type=MESH,
        )
        copy.start()
        pending.append(copy)
        cond_copies[f][at] = copy

    def cond_send_block(f, block, slot, part, peer, at):
        cond_start(f, snd_buf.at[f, block_rows(block, part)], slot, part, peer, at)

    def cond_part(f, both, block):
        rows = block_rows(block)
        snd_buf[f, rows, :] = dot(mel[rows, :], both, ((1,), (1,))).astype(BF16)

    def sum_copy(f, source, slot, peer, at):
        copy = pltpu.make_async_remote_copy(
            src_ref=source,
            dst_ref=sum_buf.at[f, slot],
            send_sem=sum_send.at[f, at],
            recv_sem=sum_recv.at[f, at],
            device_id={"dp": peer},
            device_id_type=MESH,
        )
        copy.start()
        return copy

    def sum_relay(f):
        if n_dp != 4:
            return
        sum_copies[f][0].wait_recv()
        pair = sum_buf[f, me].astype(F32) + sum_buf[f, side].astype(F32)
        sum_buf[f, far] = pair.astype(BF16)
        copy = sum_copy(f, sum_buf.at[f, far], diag, far, 1)
        sum_copies[f].append(copy)
        pending.append(copy)

    def cond_relay(f):
        if n_dp != 4:
            return
        top = tops[f]
        cond_copies[f][0].wait_recv()
        total = snd_buf[f, block_rows(far, top), :].astype(F32) + rcv_buf[f, 0, pl.ds(*top)].astype(F32)
        fwd_buf[f, pl.ds(*top)] = total.astype(BF16)
        cond_start(f, fwd_buf.at[f, pl.ds(*top)], 2, top, far, 2)

    grad_state = obj_scale * x_state
    sum_copies = [None] * NFLOW
    cond_copies = [{} for _ in range(NFLOW)]
    for f in reversed(range(NFLOW)):
        mixed, stacked, slope_tanh, slope_sigm, gated, gain = saved[f]
        grad_second = grad_state[H:]
        grad_log = grad_second * gain * mixed[H:] - obj_scale
        grad_coupling = jnp.where(
            valid, jnp.concatenate([grad_log, grad_second], axis=0), 0.0
        )
        grad_gated = dot_tn(b_skip[f], grad_coupling)
        grad_tanh = (grad_gated * slope_tanh).astype(BF16)
        grad_sigm = (grad_gated * slope_sigm).astype(BF16)
        both = jnp.concatenate([grad_tanh, grad_sigm], axis=0)
        if f > 0:
            back = fold_rows(dot(cat_rows(w_eff[f]), both, ((1,), (0,))))
            part = (
                back[8:16]
                + pltpu.roll(jnp.where(prev_mask, back[0:8], 0.0), slots - 1, 1)
                + pltpu.roll(jnp.where(next_mask, back[16:24], 0.0), 1, 1)
            )
            copies = chan_start(back_buf, NFLOW + f - 1, fold_lanes(part[:H]))
        def send_sums(f):
            left = cat_rows(jnp.concatenate([stacked, grad_coupling], axis=0))
            values = jnp.concatenate([both, gated], axis=0)
            r = fold_rows(dot(left, values, ((1,), (1,))))
            n_part = jnp.concatenate([r[0:4], r[8:12], r[16:20]], axis=0)[:, : 2 * width]
            m_part = jnp.concatenate([r[24:28, 2 * width :], r[28:32, 2 * width :]], axis=1)
            sum_buf[f, me] = jnp.concatenate([n_part, m_part], axis=0).astype(BF16)
            relay = False
            sum_copies[f] = [
                sum_copy(f, sum_buf.at[f, me], me, peer, at)
                for at, peer in enumerate(
                    [side] if relay else [lax.rem(me + step, n_dp) for step in range(1, n_dp)]
                )
            ]
            pending.extend(sum_copies[f])

        if f == NFLOW - 1:
            dp_ready()
        else:
            send_sums(f)
        if n_dp == 4:
            cond_part(f, both, diag)
            cond_send_block(f, diag, 0, tops[f], side, 0)
            cond_send_block(f, diag, 3, lows[f], diag, 4)
        if n_dp == 4:
            cond_part(f, both, far)
            cond_send_block(f, far, 2, lows[f], far, 3)
            cond_part(f, both, side)
            cond_send_block(f, side, 1, whole, side, 1)
            cond_part(f, both, me)
        else:
            snd_buf[f] = dot(mel[...], both, ((1,), (1,))).astype(BF16)
            for step in range(1, n_dp):
                peer = lax.rem(me + step, n_dp)
                cond_send_block(f, peer, step - 1, whole, peer, step - 1)
        if f == NFLOW - 1:
            send_sums(f)
        if f > 0:
            grad_first = grad_state[:H] + spread_lanes(chan_finish(back_buf, copies))
            inner = jnp.concatenate([grad_first, grad_second * gain], axis=0)
            grad_state = jnp.where(valid, dot_tn(mixes[f], inner), 0.0)

    fin_copies = [None] * NFLOW

    def weight_sums(f):
        for copy in sum_copies[f]:
            copy.wait_recv()
        total = sum_buf[f, 0].astype(F32)
        for block in range(1, n_dp):
            total = total + sum_buf[f, block].astype(F32)
        start_part = jnp.zeros((H, res_size), F32)
        n_rows = cat_rows(total)
        ends = jnp.concatenate([total[12:16, :width], total[12:16, width:]], axis=0)
        for tap in range(3):
            block = columns(
                lambda c: w_in[f, :, :, c].reshape(2 * width, c.size if isinstance(c, pl.Slice) else res),
                tap * res,
                me * res_size,
                res_size,
                res,
            )
            r = fold_rows(dot(n_rows, block, ((1,), (0,))))
            start_part = start_part + r[tap * H : tap * H + H]
        block = columns(lambda c: w_skip[f, :, c], 0, me * res_size, res_size, res)
        rows = cat_rows(ends)
        end_part = fold_rows(dot(rows, block, ((1,), (0,))))
        final = jnp.concatenate([start_part, jnp.zeros((8 - H, res_size), F32), end_part], axis=0)
        fin_copies[f] = chan_start(fin_buf.at[f], 2 * NFLOW - 1 + f, final)
        cols = columns_f32(lambda c: basis[f, :, c], me * in_size, in_size, 3 * res)
        o_in[f] = dot_tn(total, cols).reshape(2, width, in_size)
        end_cols = columns_f32(lambda c: w_end_ref[f, :, c], me * res_size, res_size, res)
        o_skip[f] = dot_tn(ends, end_cols)

    def cond_sums(f):
        if n_dp == 4:
            pieces = [(lows[f], {1: 1, 3: 2, 4: 3}), (tops[f], {1: 1, 2: 2})]
        else:
            pieces = [(whole, {at: at for at in range(n_dp - 1)})]
        waited = set()
        for part, slots_of in pieces:
            total = snd_buf[f, block_rows(me, part), :].astype(F32)
            for at, slot in slots_of.items():
                if at not in waited:
                    cond_copies[f][at].wait_recv()
                    waited.add(at)
                total = total + rcv_buf[f, slot, pl.ds(*part)].astype(F32)
            start = part[0]
            rows = min(part[1], o_cond.shape[2] - start)
            o_cond[f, 0, start : start + rows] = total[:rows, :width]
            o_cond[f, 1, start : start + rows] = total[:rows, width:]

    weight_sums(1)
    cond_relay(0)
    cond_relay(1)
    weight_sums(0)
    cond_sums(1)
    for f in reversed(range(NFLOW)):
        final = chan_finish(fin_buf.at[f], fin_copies[f])
        o_start[f] = final[:H]
        o_end[f] = final[8:16]
    cond_sums(0)
    for copy in pending:
        copy.wait_send()


def finish(i_start, i_in, i_cond, i_skip, i_end, o_start, o_in, o_cond, o_skip, o_end, sem):
    copies = [
        pltpu.make_async_copy(src, dst, sem.at[at])
        for at, (src, dst) in enumerate(
            [(i_in, o_in), (i_cond, o_cond), (i_skip, o_skip), (i_end, o_end), (i_start, o_start)]
        )
    ]
    for copy in copies:
        copy.start()
    for copy in copies:
        copy.wait()


def on_device(
    audio,
    mel,
    crop_len,
    pack_offset,
    low_mix,
    up_mix,
    log_scale,
    w_start,
    w_in,
    w_cond,
    w_skip,
    w_end,
):
    n_dp = lax.axis_size("dp")
    n_chan = lax.axis_size("chan")
    groups, _, slots = audio.shape
    channels = mel.shape[0]
    _, _, width, taps = w_in.shape
    res = w_end.shape[2]
    audio = audio.reshape(groups, slots)
    mel = mel.reshape(channels, slots)
    rows = channels // n_dp
    padded = -(-rows // 16) * 16
    if padded != rows:
        mel = jnp.pad(mel.reshape(n_dp, rows, slots), ((0, 0), (0, padded - rows), (0, 0)))
        mel = mel.reshape(n_dp * padded, slots)
        w_cond = jnp.pad(
            w_cond.reshape(NFLOW, 2, width, n_dp, rows),
            ((0, 0), (0, 0), (0, 0), (0, 0), (0, padded - rows)),
        ).reshape(NFLOW, 2, width, n_dp * padded)
    vmem = pl.BlockSpec(memory_space=pltpu.VMEM)
    hbm = pl.BlockSpec(memory_space=pltpu.HBM)
    res_size = res // n_dp
    out_shape = (
        jax.ShapeDtypeStruct((NFLOW, H, res_size), F32),
        jax.ShapeDtypeStruct((NFLOW, 2, width, taps // n_dp), F32),
        jax.ShapeDtypeStruct((NFLOW, 2, rows, width), F32),
        jax.ShapeDtypeStruct((NFLOW, width, res_size), F32),
        jax.ShapeDtypeStruct((NFLOW, 2 * H, res_size), F32),
    )
    results = pl.pallas_call(
        functools.partial(kernel, n_dp, n_chan),
        out_shape=out_shape,
        in_specs=[hbm] * 11,
        out_specs=[vmem] * 5,
        scratch_shapes=[
            pltpu.SMEM(crop_len.shape, jnp.int32),
            pltpu.VMEM(audio.shape, BF16),
            pltpu.VMEM(low_mix.shape, F32),
            pltpu.VMEM(up_mix.shape, F32),
            pltpu.VMEM(log_scale.shape, F32),
            pltpu.VMEM(w_start.shape, F32),
            pltpu.VMEM(w_end.shape, F32),
            pltpu.VMEM(mel.shape, BF16),
            pltpu.VMEM(w_in.shape, BF16),
            pltpu.VMEM(w_cond.shape, BF16),
            pltpu.VMEM(w_skip.shape, BF16),
            pltpu.VMEM((NFLOW, 8, res), F32),
            pltpu.VMEM((NFLOW, 16, 3 * res), F32),
            pltpu.VMEM((NFLOW, 2 * width, slots), F32),
            pltpu.VMEM((NFLOW, n_chan, 16, slots // 2), BF16),
            pltpu.VMEM((n_chan, 8, slots // 2), F32),
            pltpu.VMEM((NFLOW, n_chan, 16, res_size), F32),
            pltpu.VMEM((NFLOW, n_dp, 16, 2 * width), BF16),
            pltpu.VMEM((NFLOW, n_dp * padded, 2 * width), BF16),
            pltpu.VMEM((NFLOW, max(n_dp - 1, 4), padded, 2 * width), BF16),
            pltpu.VMEM((NFLOW, padded, 2 * width), BF16),
            pltpu.SemaphoreType.DMA((13,)),
            pltpu.SemaphoreType.DMA((3 * NFLOW - 1, n_chan)),
            pltpu.SemaphoreType.DMA((3 * NFLOW - 1, n_chan)),
            pltpu.SemaphoreType.DMA((NFLOW, n_dp)),
            pltpu.SemaphoreType.DMA((NFLOW, n_dp)),
            pltpu.SemaphoreType.DMA((NFLOW, max(n_dp, 5))),
            pltpu.SemaphoreType.DMA((NFLOW, max(n_dp, 5))),
            pltpu.SemaphoreType.REGULAR((2,)),
        ],
        compiler_params=pltpu.CompilerParams(
            collective_id=0, has_side_effects=True, vmem_limit_bytes=24 * 1024 * 1024
        ),
        name="flow_steps",
    )(*[
        pltpu.with_memory_space_constraint(a, pltpu.HBM)
        for a in (
            crop_len, audio, low_mix, up_mix, log_scale, w_start, w_end, mel, w_in, w_cond, w_skip
        )
    ])
    g_start, g_in, g_cond, g_skip, g_end = pl.pallas_call(
        finish,
        out_shape=out_shape,
        in_specs=[vmem] * 5,
        out_specs=[hbm] * 5,
        scratch_shapes=[pltpu.SemaphoreType.DMA((5,))],
        compiler_params=pltpu.CompilerParams(vmem_limit_bytes=16 * 1024 * 1024),
        name="finish",
    )(*results)
    return g_start, g_in, jnp.swapaxes(g_cond, 2, 3), g_skip, g_end


def solution(mesh):
    in_specs = (
        P(None, ("group", "dp"), None),
        P(None, ("group", "dp"), None),
        P("group", None),
        P("group", None),
        P(),
        P(),
        P(),
        P(),
        P(None, None, "chan", None),
        P(None, None, "chan", None),
        P(None, "chan", None),
        P(),
    )
    out_specs = (
        P("group", None, "dp"),
        P("group", None, "chan", "dp"),
        P("group", None, "chan", "dp"),
        P("group", "chan", "dp"),
        P("group", None, "dp"),
    )
    return jax.shard_map(
        on_device, mesh=mesh, in_specs=in_specs, out_specs=out_specs, check_vma=False
    )
```

```python
import functools
import math

import jax
import jax.numpy as jnp
from jax import lax
from jax.experimental import pallas as pl
from jax.experimental.pallas import tpu as pltpu
from jax.sharding import PartitionSpec as P

H = 4
NFLOW = 2
PACK = 256
MESH = pl.DeviceIdType.MESH
F32 = jnp.float32
BF16 = jnp.bfloat16


def dot(a, b, dims):
    return lax.dot_general(a, b, (dims, ((), ())), preferred_element_type=F32)


def halves(a):
    high = a.astype(BF16).astype(F32)
    return high, a - high


def cat_left(a):
    high, low = halves(a)
    return jnp.concatenate([high, high, low], axis=0).astype(BF16)


def cat_right(b):
    high, low = halves(b)
    return jnp.concatenate([high, low, high], axis=0).astype(BF16)


def dot_tn(a, b):
    return dot(cat_left(a), cat_right(b), ((0,), (0,)))


def cat_rows(a):
    high, low = halves(a)
    return jnp.concatenate([high, low], axis=0).astype(BF16)


def fold_rows(r):
    half = r.shape[0] // 2
    return r[:half] + r[half:]


def fold_lanes(a):
    half = a.shape[1] // 2
    return jnp.concatenate([a[:, :half], a[:, half:]], axis=0)


def spread_lanes(a):
    half = a.shape[0] // 2
    return jnp.concatenate([a[:half], a[half:]], axis=1)


def columns(read, base, start, size, full):
    if size % 128 == 0:
        return read(pl.ds(pl.multiple_of(base + start, 128), size))
    row = lax.broadcasted_iota(jnp.int32, (full, size), 0)
    col = lax.broadcasted_iota(jnp.int32, (full, size), 1)
    pick = jnp.where(row == col + start, 1.0, 0.0).astype(BF16)
    return dot(read(slice(base, base + full)), pick, ((1,), (0,))).astype(BF16)


def columns_f32(read, start, size, full):
    if size % 128 == 0:
        return read(pl.ds(pl.multiple_of(start, 128), size))
    row = lax.broadcasted_iota(jnp.int32, (full, size), 0)
    col = lax.broadcasted_iota(jnp.int32, (full, size), 1)
    pick = jnp.where(row == col + start, 1.0, 0.0).astype(BF16)
    return fold_rows(dot(cat_rows(read(slice(None))), pick, ((1,), (0,))))


def kernel(
    n_dp,
    n_chan,
    len_hbm,
    audio_hbm,
    low_hbm,
    up_hbm,
    scale_hbm,
    w_start_hbm,
    w_end_hbm,
    mel_hbm,
    w_in_hbm,
    w_cond_hbm,
    w_skip_hbm,
    o_start,
    o_in,
    o_cond,
    o_skip,
    o_end,
    len_ref,
    audio_ref,
    low_ref,
    up_ref,
    scale_ref,
    w_start_ref,
    w_end_ref,
    mel,
    w_in,
    w_cond,
    w_skip,
    w_first,
    basis,
    cond,
    chan_buf,
    back_buf,
    fin_buf,
    sum_buf,
    snd_buf,
    rcv_buf,
    fwd_buf,
    load_sem,
    chan_send,
    chan_recv,
    sum_send,
    sum_recv,
    cond_send,
    cond_recv,
    go,
):
    slots = audio_ref.shape[1]
    cap = slots // n_dp
    width = w_in_hbm.shape[2]
    res = w_end_ref.shape[2]
    mel_rows = mel_hbm.shape[0] // n_dp
    res_size = o_skip.shape[2]
    in_size = o_in.shape[3]
    obj_scale = 8.0 / math.sqrt(n_dp * PACK)
    me = lax.axis_index("dp")
    chan = lax.axis_index("chan")

    barrier = pltpu.get_barrier_semaphore()
    split = n_chan == 4
    core = lax.rem(chan, 2)
    even, odd = chan - core, chan - core + 1

    def signal(semaphore, **device):
        pl.semaphore_signal(semaphore, inc=1, device_id=device, device_id_type=MESH)

    if split:
        signal(barrier, chan=lax.rem(even + 2, n_chan))

        @pl.when(core == 1)
        def _():
            signal(barrier, chan=even)
    else:
        for step in range(1, n_chan):
            signal(barrier, chan=lax.rem(chan + step, n_chan))
        for step in range(1, n_dp):
            signal(barrier, dp=lax.rem(me + step, n_dp))

    def chan_ready():
        if not split:
            pl.semaphore_wait(barrier, n_chan + n_dp - 2)
            return

        @pl.when(core == 0)
        def _():
            pl.semaphore_wait(barrier, n_chan - 1)
            signal(go.at[0], chan=odd)

        @pl.when(core == 1)
        def _():
            pl.semaphore_wait(go.at[0], 1)

    def dp_ready():
        if not split:
            return

        @pl.when(core == 1)
        def _():
            pl.semaphore_wait(barrier, 2 * (n_dp - 1))
            signal(go.at[1], chan=even)

        @pl.when(core == 0)
        def _():
            pl.semaphore_wait(go.at[1], 1)

    pairs = {
        "len": (len_hbm, len_ref),
        "audio": (audio_hbm, audio_ref),
        "low": (low_hbm, low_ref),
        "up": (up_hbm, up_ref),
        "scale": (scale_hbm, scale_ref),
        "start": (w_start_hbm, w_start_ref),
        "in0": (w_in_hbm.at[0], w_in.at[0]),
        "end": (w_end_hbm, w_end_ref),
        "skip": (w_skip_hbm, w_skip),
        "mel": (mel_hbm, mel),
        "cond0": (w_cond_hbm.at[0], w_cond.at[0]),
        "in1": (w_in_hbm.at[1], w_in.at[1]),
        "cond1": (w_cond_hbm.at[1], w_cond.at[1]),
    }
    loads = {
        key: pltpu.make_async_copy(src, dst, load_sem.at[at])
        for at, (key, (src, dst)) in enumerate(pairs.items())
    }
    for load in loads.values():
        load.start()
    if split:
        for step in range(1, n_dp):
            signal(barrier, dp=lax.rem(me + step, n_dp), chan=odd)

    def chan_start(buf, phase, value):
        buf[chan] = value
        copies = [
            pltpu.make_async_remote_copy(
                src_ref=buf.at[chan],
                dst_ref=buf.at[chan],
                send_sem=chan_send.at[phase, step],
                recv_sem=chan_recv.at[phase, step],
                device_id={"chan": lax.rem(chan + step, n_chan)},
                device_id_type=MESH,
            )
            for step in sorted(range(1, n_chan), key=lambda step: abs(2 * step - n_chan))
        ]
        for copy in copies:
            copy.start()
        pending.extend(copies)
        return copies

    def chan_finish(buf, copies):
        for copy in copies:
            copy.wait_recv()
        total = buf[0].astype(F32)
        for block in range(1, n_chan):
            total = total + buf[block].astype(F32)
        return total

    pending = []
    w_first[...] = jnp.zeros(w_first.shape, F32)
    basis[...] = jnp.zeros(basis.shape, F32)

    for key in ("len", "audio", "low", "up", "scale"):
        loads[key].wait()
    column = lax.broadcasted_iota(jnp.int32, (8, slots), 1)
    owner = column // cap
    within = column - owner * cap
    lens = jnp.zeros((8, slots), jnp.int32)
    for block in range(n_dp):
        lens = jnp.where(owner == block, len_ref[block, me], lens)
    valid = within < lens
    prev_mask = valid & (within >= 1)
    next_mask = within + 1 < lens

    row8 = lax.broadcasted_iota(jnp.int32, (8, 8), 0)
    col8 = lax.broadcasted_iota(jnp.int32, (8, 8), 1)
    mixes = []
    for f in range(NFLOW):
        lower = jnp.where(row8 > col8, low_ref[f], jnp.where(row8 == col8, 1.0, 0.0))
        diag = jnp.broadcast_to(jnp.exp(scale_ref[f : f + 1, :]), (8, 8))
        upper = jnp.where(row8 < col8, up_ref[f], jnp.where(row8 == col8, diag, 0.0))
        mixing = lower[:, 0:1] * upper[0:1, :]
        for k in range(1, 8):
            mixing = mixing + lower[:, k : k + 1] * upper[k : k + 1, :]
        mixes.append(mixing)

    def mix(f, x):
        mixing = mixes[f]
        mixed = mixing[:, 0:1] * x[0:1, :]
        for k in range(1, 8):
            mixed = mixed + mixing[:, k : k + 1] * x[k : k + 1, :]
        return mixed

    w_eff = [None] * NFLOW
    b_skip = [None] * NFLOW

    def precompute(f):
        loads["in%d" % f].wait()
        start16 = cat_rows(w_first[f])
        taps = []
        for tap in range(3):
            block = w_in[f, :, :, tap * res : (tap + 1) * res].reshape(2 * width, res)
            taps.append(fold_rows(dot(start16, block, ((1,), (1,)))))
        w_eff[f] = jnp.concatenate(taps, axis=0)
        if f == 0:
            loads["end"].wait()
            loads["skip"].wait()
        b_skip[f] = fold_rows(dot(cat_rows(w_end_ref[f]), w_skip[f], ((1,), (1,))))
        if f == 0:
            loads["mel"].wait()
        loads["cond%d" % f].wait()
        every = w_cond[f].reshape(2 * width, w_cond.shape[3])
        cond[f] = dot(every, mel[...], ((1,), (0,)))

    x_state = jnp.where(valid, audio_ref[...].astype(F32), 0.0)
    loads["start"].wait()
    for f in range(NFLOW):
        w_first[f, :H] = w_start_ref[f]
    precompute(0)
    saved = []
    for f in range(NFLOW):
        mixed = mix(f, x_state)
        stacked = jnp.concatenate(
            [
                jnp.where(prev_mask, pltpu.roll(mixed, 1, 1), 0.0),
                mixed,
                jnp.where(next_mask, pltpu.roll(mixed, slots - 1, 1), 0.0),
            ],
            axis=0,
        )
        pre = dot_tn(w_eff[f], stacked) + cond[f]
        tanh_val = jnp.tanh(pre[:width])
        sigm_val = 0.5 * jnp.tanh(0.5 * pre[width:]) + 0.5
        gated = (tanh_val * sigm_val).astype(BF16)
        part = fold_rows(dot(cat_rows(b_skip[f]), gated, ((1,), (0,))))
        if f == 0:
            chan_ready()
        copies = chan_start(chan_buf.at[f], f, fold_lanes(part).astype(BF16))
        if f == 0:
            precompute(1)
            for g in range(NFLOW):
                for tap in range(3):
                    basis[g, tap * H : tap * H + H, tap * res : (tap + 1) * res] = w_start_ref[g]
        slope_tanh = sigm_val * (1.0 - tanh_val * tanh_val)
        slope_sigm = tanh_val * sigm_val * (1.0 - sigm_val)
        coupling = spread_lanes(chan_finish(chan_buf.at[f], copies))
        gain = jnp.exp(coupling[:H])
        second = mixed[H:]
        saved.append((mixed, stacked, slope_tanh, slope_sigm, gated, gain))
        x_state = jnp.where(
            valid, jnp.concatenate([mixed[:H], gain * second + coupling[H:]], axis=0), 0.0
        )

    side = me + 1 - 2 * lax.rem(me, 2)
    far = lax.rem(me + 2, n_dp)
    diag = lax.rem(side + 2, n_dp)
    tops = [(0, mel_rows * 64 // 160 // 16 * 16), (0, mel_rows * 80 // 160 // 16 * 16)]
    lows = [(size, mel_rows - size) for _, size in tops]
    whole = (0, mel_rows)

    def block_rows(block, part=whole):
        start, size = part
        return pl.ds(pl.multiple_of(block * mel_rows + start, 16), size)

    def cond_start(f, source, slot, part, peer, at):
        copy = pltpu.make_async_remote_copy(
            src_ref=source,
            dst_ref=rcv_buf.at[f, slot, pl.ds(*part)],
            send_sem=cond_send.at[f, at],
            recv_sem=cond_recv.at[f, at],
            device_id={"dp": peer},
            device_id_type=MESH,
        )
        copy.start()
        pending.append(copy)
        cond_copies[f][at] = copy

    def cond_send_block(f, block, slot, part, peer, at):
        cond_start(f, snd_buf.at[f, block_rows(block, part)], slot, part, peer, at)

    def cond_part(f, both, block):
        rows = block_rows(block)
        snd_buf[f, rows, :] = dot(mel[rows, :], both, ((1,), (1,))).astype(BF16)

    def sum_copy(f, source, slot, peer, at):
        copy = pltpu.make_async_remote_copy(
            src_ref=source,
            dst_ref=sum_buf.at[f, slot],
            send_sem=sum_send.at[f, at],
            recv_sem=sum_recv.at[f, at],
            device_id={"dp": peer},
            device_id_type=MESH,
        )
        copy.start()
        return copy

    def sum_relay(f):
        if n_dp != 4:
            return
        sum_copies[f][0].wait_recv()
        pair = sum_buf[f, me].astype(F32) + sum_buf[f, side].astype(F32)
        sum_buf[f, far] = pair.astype(BF16)
        copy = sum_copy(f, sum_buf.at[f, far], diag, far, 1)
        sum_copies[f].append(copy)
        pending.append(copy)

    def cond_relay(f):
        if n_dp != 4:
            return
        top = tops[f]
        cond_copies[f][0].wait_recv()
        total = snd_buf[f, block_rows(far, top), :].astype(F32) + rcv_buf[f, 0, pl.ds(*top)].astype(F32)
        fwd_buf[f, pl.ds(*top)] = total.astype(BF16)
        cond_start(f, fwd_buf.at[f, pl.ds(*top)], 2, top, far, 2)

    grad_state = obj_scale * x_state
    sum_copies = [None] * NFLOW
    cond_copies = [{} for _ in range(NFLOW)]
    for f in reversed(range(NFLOW)):
        mixed, stacked, slope_tanh, slope_sigm, gated, gain = saved[f]
        grad_second = grad_state[H:]
        grad_log = grad_second * gain * mixed[H:] - obj_scale
        grad_coupling = jnp.where(
            valid, jnp.concatenate([grad_log, grad_second], axis=0), 0.0
        )
        grad_gated = dot_tn(b_skip[f], grad_coupling)
        grad_tanh = (grad_gated * slope_tanh).astype(BF16)
        grad_sigm = (grad_gated * slope_sigm).astype(BF16)
        both = jnp.concatenate([grad_tanh, grad_sigm], axis=0)
        if f > 0:
            back = fold_rows(dot(cat_rows(w_eff[f]), both, ((1,), (0,))))
            part = (
                back[8:16]
                + pltpu.roll(jnp.where(prev_mask, back[0:8], 0.0), slots - 1, 1)
                + pltpu.roll(jnp.where(next_mask, back[16:24], 0.0), 1, 1)
            )
            copies = chan_start(back_buf, NFLOW + f - 1, fold_lanes(part[:H]))
        left = cat_rows(jnp.concatenate([stacked, grad_coupling], axis=0))
        values = jnp.concatenate([both, gated], axis=0)
        r = fold_rows(dot(left, values, ((1,), (1,))))
        n_part = jnp.concatenate([r[0:4], r[8:12], r[16:20]], axis=0)[:, : 2 * width]
        m_part = jnp.concatenate([r[24:28, 2 * width :], r[28:32, 2 * width :]], axis=1)
        sum_buf[f, me] = jnp.concatenate([n_part, m_part], axis=0).astype(BF16)
        if f == NFLOW - 1:
            dp_ready()
        relay = False
        sum_copies[f] = [
            sum_copy(f, sum_buf.at[f, me], me, peer, at)
            for at, peer in enumerate(
                [side] if relay else [lax.rem(me + step, n_dp) for step in range(1, n_dp)]
            )
        ]
        pending += sum_copies[f]
        if n_dp == 4:
            cond_part(f, both, diag)
            cond_send_block(f, diag, 0, tops[f], side, 0)
            cond_send_block(f, diag, 3, lows[f], diag, 4)
        if n_dp == 4:
            cond_part(f, both, far)
            cond_send_block(f, far, 2, lows[f], far, 3)
            cond_part(f, both, side)
            cond_send_block(f, side, 1, whole, side, 1)
            cond_part(f, both, me)
        else:
            snd_buf[f] = dot(mel[...], both, ((1,), (1,))).astype(BF16)
            for step in range(1, n_dp):
                peer = lax.rem(me + step, n_dp)
                cond_send_block(f, peer, step - 1, whole, peer, step - 1)
        if f > 0:
            grad_first = grad_state[:H] + spread_lanes(chan_finish(back_buf, copies))
            inner = jnp.concatenate([grad_first, grad_second * gain], axis=0)
            grad_state = jnp.where(valid, dot_tn(mixes[f], inner), 0.0)

    fin_copies = [None] * NFLOW

    def weight_sums(f):
        for copy in sum_copies[f]:
            copy.wait_recv()
        total = sum_buf[f, 0].astype(F32)
        for block in range(1, n_dp):
            total = total + sum_buf[f, block].astype(F32)
        start_part = jnp.zeros((H, res_size), F32)
        n_rows = cat_rows(total)
        ends = jnp.concatenate([total[12:16, :width], total[12:16, width:]], axis=0)
        for tap in range(3):
            block = columns(
                lambda c: w_in[f, :, :, c].reshape(2 * width, c.size if isinstance(c, pl.Slice) else res),
                tap * res,
                me * res_size,
                res_size,
                res,
            )
            r = fold_rows(dot(n_rows, block, ((1,), (0,))))
            start_part = start_part + r[tap * H : tap * H + H]
        block = columns(lambda c: w_skip[f, :, c], 0, me * res_size, res_size, res)
        rows = cat_rows(ends)
        end_part = fold_rows(dot(rows, block, ((1,), (0,))))
        final = jnp.concatenate([start_part, jnp.zeros((8 - H, res_size), F32), end_part], axis=0)
        fin_copies[f] = chan_start(fin_buf.at[f], 2 * NFLOW - 1 + f, final)
        cols = columns_f32(lambda c: basis[f, :, c], me * in_size, in_size, 3 * res)
        o_in[f] = dot_tn(total, cols).reshape(2, width, in_size)
        end_cols = columns_f32(lambda c: w_end_ref[f, :, c], me * res_size, res_size, res)
        o_skip[f] = dot_tn(ends, end_cols)

    def cond_sums(f):
        if n_dp == 4:
            pieces = [(lows[f], {1: 1, 3: 2, 4: 3}), (tops[f], {1: 1, 2: 2})]
        else:
            pieces = [(whole, {at: at for at in range(n_dp - 1)})]
        waited = set()
        for part, slots_of in pieces:
            total = snd_buf[f, block_rows(me, part), :].astype(F32)
            for at, slot in slots_of.items():
                if at not in waited:
                    cond_copies[f][at].wait_recv()
                    waited.add(at)
                total = total + rcv_buf[f, slot, pl.ds(*part)].astype(F32)
            start = part[0]
            rows = min(part[1], o_cond.shape[2] - start)
            o_cond[f, 0, start : start + rows] = total[:rows, :width]
            o_cond[f, 1, start : start + rows] = total[:rows, width:]

    cond_relay(1)
    weight_sums(1)
    cond_relay(0)
    weight_sums(0)
    cond_sums(1)
    for f in reversed(range(NFLOW)):
        final = chan_finish(fin_buf.at[f], fin_copies[f])
        o_start[f] = final[:H]
        o_end[f] = final[8:16]
    cond_sums(0)
    for copy in pending:
        copy.wait_send()


def finish(i_start, i_in, i_cond, i_skip, i_end, o_start, o_in, o_cond, o_skip, o_end, sem):
    copies = [
        pltpu.make_async_copy(src, dst, sem.at[at])
        for at, (src, dst) in enumerate(
            [(i_in, o_in), (i_cond, o_cond), (i_skip, o_skip), (i_end, o_end), (i_start, o_start)]
        )
    ]
    for copy in copies:
        copy.start()
    for copy in copies:
        copy.wait()


def on_device(
    audio,
    mel,
    crop_len,
    pack_offset,
    low_mix,
    up_mix,
    log_scale,
    w_start,
    w_in,
    w_cond,
    w_skip,
    w_end,
):
    n_dp = lax.axis_size("dp")
    n_chan = lax.axis_size("chan")
    groups, _, slots = audio.shape
    channels = mel.shape[0]
    _, _, width, taps = w_in.shape
    res = w_end.shape[2]
    audio = audio.reshape(groups, slots)
    mel = mel.reshape(channels, slots)
    rows = channels // n_dp
    padded = -(-rows // 16) * 16
    if padded != rows:
        mel = jnp.pad(mel.reshape(n_dp, rows, slots), ((0, 0), (0, padded - rows), (0, 0)))
        mel = mel.reshape(n_dp * padded, slots)
        w_cond = jnp.pad(
            w_cond.reshape(NFLOW, 2, width, n_dp, rows),
            ((0, 0), (0, 0), (0, 0), (0, 0), (0, padded - rows)),
        ).reshape(NFLOW, 2, width, n_dp * padded)
    vmem = pl.BlockSpec(memory_space=pltpu.VMEM)
    hbm = pl.BlockSpec(memory_space=pltpu.HBM)
    res_size = res // n_dp
    out_shape = (
        jax.ShapeDtypeStruct((NFLOW, H, res_size), F32),
        jax.ShapeDtypeStruct((NFLOW, 2, width, taps // n_dp), F32),
        jax.ShapeDtypeStruct((NFLOW, 2, rows, width), F32),
        jax.ShapeDtypeStruct((NFLOW, width, res_size), F32),
        jax.ShapeDtypeStruct((NFLOW, 2 * H, res_size), F32),
    )
    results = pl.pallas_call(
        functools.partial(kernel, n_dp, n_chan),
        out_shape=out_shape,
        in_specs=[hbm] * 11,
        out_specs=[vmem] * 5,
        scratch_shapes=[
            pltpu.SMEM(crop_len.shape, jnp.int32),
            pltpu.VMEM(audio.shape, BF16),
            pltpu.VMEM(low_mix.shape, F32),
            pltpu.VMEM(up_mix.shape, F32),
            pltpu.VMEM(log_scale.shape, F32),
            pltpu.VMEM(w_start.shape, F32),
            pltpu.VMEM(w_end.shape, F32),
            pltpu.VMEM(mel.shape, BF16),
            pltpu.VMEM(w_in.shape, BF16),
            pltpu.VMEM(w_cond.shape, BF16),
            pltpu.VMEM(w_skip.shape, BF16),
            pltpu.VMEM((NFLOW, 8, res), F32),
            pltpu.VMEM((NFLOW, 16, 3 * res), F32),
            pltpu.VMEM((NFLOW, 2 * width, slots), F32),
            pltpu.VMEM((NFLOW, n_chan, 16, slots // 2), BF16),
            pltpu.VMEM((n_chan, 8, slots // 2), F32),
            pltpu.VMEM((NFLOW, n_chan, 16, res_size), F32),
            pltpu.VMEM((NFLOW, n_dp, 16, 2 * width), BF16),
            pltpu.VMEM((NFLOW, n_dp * padded, 2 * width), BF16),
            pltpu.VMEM((NFLOW, max(n_dp - 1, 4), padded, 2 * width), BF16),
            pltpu.VMEM((NFLOW, padded, 2 * width), BF16),
            pltpu.SemaphoreType.DMA((13,)),
            pltpu.SemaphoreType.DMA((3 * NFLOW - 1, n_chan)),
            pltpu.SemaphoreType.DMA((3 * NFLOW - 1, n_chan)),
            pltpu.SemaphoreType.DMA((NFLOW, n_dp)),
            pltpu.SemaphoreType.DMA((NFLOW, n_dp)),
            pltpu.SemaphoreType.DMA((NFLOW, max(n_dp, 5))),
            pltpu.SemaphoreType.DMA((NFLOW, max(n_dp, 5))),
            pltpu.SemaphoreType.REGULAR((2,)),
        ],
        compiler_params=pltpu.CompilerParams(
            collective_id=0, has_side_effects=True, vmem_limit_bytes=24 * 1024 * 1024
        ),
        name="flow_steps",
    )(*[
        pltpu.with_memory_space_constraint(a, pltpu.HBM)
        for a in (
            crop_len, audio, low_mix, up_mix, log_scale, w_start, w_end, mel, w_in, w_cond, w_skip
        )
    ])
    g_start, g_in, g_cond, g_skip, g_end = pl.pallas_call(
        finish,
        out_shape=out_shape,
        in_specs=[vmem] * 5,
        out_specs=[hbm] * 5,
        scratch_shapes=[pltpu.SemaphoreType.DMA((5,))],
        compiler_params=pltpu.CompilerParams(vmem_limit_bytes=16 * 1024 * 1024),
        name="finish",
    )(*results)
    return g_start, g_in, jnp.swapaxes(g_cond, 2, 3), g_skip, g_end


def solution(mesh):
    in_specs = (
        P(None, ("group", "dp"), None),
        P(None, ("group", "dp"), None),
        P("group", None),
        P("group", None),
        P(),
        P(),
        P(),
        P(),
        P(None, None, "chan", None),
        P(None, None, "chan", None),
        P(None, "chan", None),
        P(),
    )
    out_specs = (
        P("group", None, "dp"),
        P("group", None, "chan", "dp"),
        P("group", None, "chan", "dp"),
        P("group", "chan", "dp"),
        P("group", None, "dp"),
    )
    return jax.shard_map(
        on_device, mesh=mesh, in_specs=in_specs, out_specs=out_specs, check_vma=False
    )
```
